256 devices in a mesh: gx: 8 (over z), gy: 32 (over y, x, core).
Axes of the slice: x: 4, y: 4, z: 8, core: 2. Of those that a mesh axis runs over, the one named last changes fastest.
Arguments:
- velocity: float32 [3, 8, 512, 1024], P(None, 'gx', 'gy'), may hold values from -6 to 6
- y_metric: float32 [512], P('gy'), may hold values from 0.5 to 4
- forward_rate: float32 [3, 512], P(None, 'gy'), may hold values from 0.9921875 to 1
- backward_rate: float32 [3, 512], P(None, 'gy'), may hold values from 0.9921875 to 1
- pivot_inv: float32 [3, 512], P(None, 'gy'), may hold values from 0 to 0.0007324219
- particle_vel: float32 [3, 917504], P(None, ('gx', 'gy')), may hold values from -6 to 6
- particle_cell: int32 [917504], P(('gx', 'gy')), may hold values from 0 to 16383
- particle_offset: float32 [3, 917504], P(None, ('gx', 'gy')), may hold values from 0 to 1
- inverse_tau: float32 [917504], P(('gx', 'gy')), may hold values from 0.5 to 8
- outgoing_count: int32 [8, 32, 3], P('gx', 'gy'), may hold values from 0 to 512, as said below
Outputs:
- velocity_out: float32 [3, 8, 512, 1024], P(None, 'gx', 'gy')
- particle_out: float32 [3, 917504], P(None, ('gx', 'gy'))
The draws below stay inside these ranges and needn't reach their ends.
Inputs may be any that keep to these rules, and one draw needn't show every extreme that they name: `outgoing_count`: entry d of a block counts the live leading slots of its outgoing block d; the -y block of the lowest and the +y block of the highest wall-normal blocks are empty; some +x block is full.
All inputs are finite; a program needn't handle non-finite values.
Results may differ from the reference program's by a relative error of at most 0.00029.
Values sent between devices are 32-bit elements; how exact they have to be, the bound alone decides.
A program may use at most 192 MiB of HBM per device.

```python
import math
import jax
import jax.numpy as jnp
from jax import lax

CX = 1
CY = 16
CZ = 1024
RESIDENT = 2048
CAP = 512
SECTIONS = 3
NX = 8
NY = 512
NZ = 1024
CELLS = 16384
SLOTS = 3584
PARTS_SIZE = 917504
N_GX = 8
N_GY = 32


def rate_triple(key):
    first = jax.random.uniform(jax.random.fold_in(key, 11), (SECTIONS, NY), jnp.float32)
    second = jax.random.uniform(jax.random.fold_in(key, 12), (SECTIONS, NY), jnp.float32)
    third = jax.random.uniform(jax.random.fold_in(key, 13), (SECTIONS, NY), jnp.float32)
    down_strength = 0.25 * jnp.exp(jnp.log(16.0) * first)
    up_strength = 0.25 * jnp.exp(jnp.log(16.0) * second)
    gain = 3.0 * jnp.exp(jnp.log(4.0) * third)
    down_rate = jnp.exp(-down_strength / NY)
    up_rate = jnp.exp(-up_strength / NY)
    scale_rate = (1.0 - down_rate) * (1.0 - up_rate) * gain
    return (down_rate, up_rate, scale_rate)


def draw_forward_rate(key, part):
    return rate_triple(key)[0]


def draw_backward_rate(key, part):
    return rate_triple(key)[1]


def draw_pivot_inv(key, part):
    return rate_triple(key)[2]


def draw_outgoing_count(key, part):
    counts = jax.random.randint(jax.random.fold_in(key, 21), (N_GX, N_GY, 3), 0, CAP + 1)
    place_x = jax.random.randint(jax.random.fold_in(key, 22), (), 0, N_GX)
    place_y = jax.random.randint(jax.random.fold_in(key, 23), (), 0, N_GY)
    counts = counts.at[:, 0, 1].set(0)
    counts = counts.at[:, N_GY - 1, 2].set(0)
    counts = counts.at[place_x, place_y, 0].set(CAP)
    return counts.astype(jnp.int32)


def plant(drawn, key, low, top_value):
    index_at = [jax.random.randint(jax.random.fold_in(key, axis), (), 0, length) for axis, length in enumerate(drawn.shape)]
    main_axis = drawn.shape.index(max(drawn.shape))
    neighbour = index_at[:main_axis] + [(index_at[main_axis] + 1) % drawn.shape[main_axis]] + index_at[main_axis + 1:]
    return drawn.at[tuple(index_at)].set(low).at[tuple(neighbour)].set(top_value)


def levels(own_key, shape, pieces, low, largest):
    def one(axis_at, parts):
        heights = jax.random.uniform(jax.random.fold_in(jax.random.fold_in(own_key, 6), axis_at), (parts,), jnp.float32, low / len(pieces), largest / len(pieces))
        return jnp.repeat(jnp.exp(heights), shape[axis_at] // parts).reshape((-1,) + (1,) * (len(shape) - axis_at - 1))

    level = one(*pieces[0])
    for cut in pieces[1:]:
        level = level * one(*cut)
    return level


def scatter_about(stream_key, dims, deviation, reach, split=(), held_as=jnp.bfloat16):
    entries = jax.random.normal(stream_key, dims, jnp.float32) * deviation
    if len(split) > 0:
        entries = levels(stream_key, dims, split, -0.22, 0.18) * entries
    return jnp.clip(entries, min=-reach, max=reach).astype(held_as)


def setup_inputs(seed: int = 0) -> dict:
    splits = jax.random.split(jax.random.key(seed), 11)
    velocity = scatter_about(splits[0], (3, NX, NY, NZ), 1.0, 6.0, ((1, 8), (2, 32)), jnp.float32)
    y_metric = jnp.clip(jnp.exp(math.log(4.0) - 2.0794415 * jax.random.uniform(splits[1], (NY,), jnp.float32) ** levels(splits[1], (NY,), ((0, 32),), -0.2, 0.2)), 0.5, 4.0)
    forward_rate = draw_forward_rate(jax.random.fold_in(splits[10], 71), 0)
    backward_rate = draw_backward_rate(jax.random.fold_in(splits[10], 71), 0)
    pivot_inv = draw_pivot_inv(jax.random.fold_in(splits[10], 71), 0)
    particle_vel = scatter_about(splits[5], (3, PARTS_SIZE), 1.0, 6.0, ((1, 256),), jnp.float32)
    particle_cell = plant(jax.random.randint(splits[6], (PARTS_SIZE,), 0, CELLS), jax.random.fold_in(splits[6], 1), 0, CELLS - 1).astype(jnp.int32)
    particle_offset = jnp.clip(1.0 * jax.random.uniform(splits[7], (3, PARTS_SIZE), jnp.float32) ** levels(splits[7], (3, PARTS_SIZE), ((1, 256),), -0.2, 0.2), 0.0, 1.0)
    inverse_tau = jnp.clip(jnp.exp(math.log(8.0) - 2.7725887 * jax.random.uniform(splits[8], (PARTS_SIZE,), jnp.float32) ** levels(splits[8], (PARTS_SIZE,), ((0, 256),), -0.2, 0.2)), 0.5, 8.0)
    outgoing_count = draw_outgoing_count(jax.random.fold_in(splits[10], 71), 0)
    return {"velocity": velocity, "y_metric": y_metric, "forward_rate": forward_rate, "backward_rate": backward_rate, "pivot_inv": pivot_inv, "particle_vel": particle_vel, "particle_cell": particle_cell, "particle_offset": particle_offset, "inverse_tau": inverse_tau, "outgoing_count": outgoing_count}


SECTION_WEIGHTS = (8.0 / 15.0, 5.0 / 12.0, 3.0 / 4.0)
TIME_STEP = 0.3
STREAM_SCALE = 2.0
SPAN_SCALE = 2.0
COUPLING = 0.5
CORNER_LIST = ((0, 0, 0), (0, 0, 1), (0, 1, 0), (0, 1, 1), (1, 0, 0), (1, 0, 1), (1, 1, 0), (1, 1, 1))


def stencil(field, upper_x, lower_x, upper_y, lower_y, upper_z, lower_z, y_metric):
    slope_x = (upper_x - lower_x) * (0.5 * STREAM_SCALE)
    slope_y = (upper_y - lower_y) * (0.5 * y_metric)[None, None, :, None]
    slope_z = (upper_z - lower_z) * (0.5 * SPAN_SCALE)
    return -(field[0:1] * slope_x + field[1:2] * slope_y + field[2:3] * slope_z)


def corner_weight(offsets, corner):
    weight = None
    for dimension in range(3):
        factor = offsets[dimension] if corner[dimension] else 1.0 - offsets[dimension]
        weight = factor if weight is None else weight * factor
    return weight


def convect(field, y_metric):
    padded = jnp.pad(field, ((0, 0), (0, 0), (1, 1), (0, 0)))
    return stencil(field, jnp.roll(field, -1, axis=1), jnp.roll(field, 1, axis=1),
                   padded[:, :, 2:, :], padded[:, :, :-2, :],
                   jnp.roll(field, -1, axis=3), jnp.roll(field, 1, axis=3), y_metric)


def solve(rhs, down_rate, up_rate, scale_rate):
    rows = jnp.moveaxis(rhs, 2, 0)

    def downward(carry, item):
        value, rate = item
        result = value + rate * carry
        return result, result

    def upward(carry, item):
        value, rate, scale = item
        result = scale * value + rate * carry
        return result, result

    start = jnp.zeros_like(rows[0])
    _, forward = lax.scan(downward, start, (rows, down_rate))
    _, backward = lax.scan(upward, start, (forward, up_rate, scale_rate), reverse=True)
    return jnp.moveaxis(backward, 0, 2)


def reference(velocity, y_metric, forward_rate, backward_rate, pivot_inv, particle_vel, particle_cell, particle_offset, inverse_tau, outgoing_count):
    position = jnp.arange(PARTS_SIZE, dtype=jnp.int32)
    slot_num = position % SLOTS
    block = position // SLOTS
    block_x = block // N_GY
    block_y = block % N_GY
    remain = slot_num - RESIDENT
    heading = jnp.clip(remain // CAP, 0, 2)
    limit = outgoing_count[block_x, block_y, heading]
    live = jnp.where((slot_num < RESIDENT) | (remain % CAP < limit), 1.0, 0.0).astype(jnp.float32)
    cell_x = particle_cell // (CY * CZ)
    cell_y = (particle_cell // CZ) % CY
    cell_z = particle_cell % CZ
    global_x = block_x * CX + cell_x
    global_y = block_y * CY + cell_y
    flat_cell = (global_x * NY + global_y) * NZ + cell_z
    field = velocity
    moving = particle_vel
    for section_num in range(SECTIONS):
        step_size = TIME_STEP * SECTION_WEIGHTS[section_num]
        extended = jnp.concatenate([field, field[:, :1]], axis=1)
        extended = jnp.pad(extended, ((0, 0), (0, 0), (0, 1), (0, 0)))
        fluid_at = jnp.zeros_like(moving)
        for corner in CORNER_LIST:
            values = extended[:, global_x + corner[0], global_y + corner[1], (cell_z + corner[2]) % NZ]
            fluid_at = fluid_at + corner_weight(particle_offset, corner) * values
        drag = inverse_tau * (fluid_at - moving)
        moving = moving + step_size * drag
        force = jnp.zeros((3, NX * NY * NZ), jnp.float32).at[:, flat_cell].add(-COUPLING * drag * live)
        rhs = field + step_size * (convect(field, y_metric) + force.reshape(field.shape))
        field = solve(rhs, forward_rate[section_num], backward_rate[section_num], pivot_inv[section_num])
    masked = moving * live
    grid = masked.reshape(3, N_GX, N_GY, SLOTS)
    kept = grid[..., :RESIDENT]
    to_x = grid[..., RESIDENT:RESIDENT + CAP]
    to_lower = grid[..., RESIDENT + CAP:RESIDENT + 2 * CAP]
    to_upper = grid[..., RESIDENT + 2 * CAP:]
    from_x = jnp.roll(to_x, 1, axis=1)
    empty = jnp.zeros_like(to_x[:, :, :1])
    from_above = jnp.concatenate([to_lower[:, :, 1:], empty], axis=2)
    from_below = jnp.concatenate([empty, to_upper[:, :, :-1]], axis=2)
    moved = jnp.concatenate([kept, from_x, from_above, from_below], axis=3).reshape(3, PARTS_SIZE)
    return field, moved
```

```python
import functools

import jax
import jax.numpy as jnp
from jax import lax
from jax.experimental import pallas as pl
from jax.experimental.pallas import tpu as pltpu
from jax.sharding import PartitionSpec as P

RESIDENT = 2048
CAP = 512
SECTIONS = 3
SECTION_WEIGHTS = (8.0 / 15.0, 5.0 / 12.0, 3.0 / 4.0)
TIME_STEP = 0.3
STREAM_SCALE = 2.0
SPAN_SCALE = 2.0
COUPLING = 0.5
CHUNK = 512
MESH = pl.DeviceIdType.MESH
F32 = jnp.float32
BF16 = jnp.bfloat16


def row_size(lanes):
    return 8 if lanes == 32 else max(2, lanes // 2)


def halves(x):
    high = x.astype(BF16)
    return high, (x - high.astype(F32)).astype(BF16)


def kernel(
    dims,
    vel, metric, fwd, bwd, piv, pvel, cell, offset, tau, count,
    field_out, part_out,
    onehot, table, el_table, scat, accum, wts, ymask, ywt, ab, speed, fluid, live_ref, moved,
    solve_cols, carry_col, alpha, beta, ymet, unit_rows,
    part, planes, uref, rhs_ref, edge, edge_in, msg, got1, got2, own2, ans, el, mig,
    s1s, s1r, s2s, s2r, s3s, s3r, pls, plr, eds, edr, mgs, mgr,
):
    nx, lanes, rsize = dims
    rows_n = lanes // rsize
    comps, cy, cz = vel.shape
    width = cz // rsize
    slots = pvel.shape[1]
    chunk = min(CHUNK, slots)
    steps = slots // chunk
    last = cy - 1
    gx = lax.axis_index("gx")
    gy = lax.axis_index("gy")
    place = lax.rem(gy, rsize)
    line = gy // rsize
    line0 = line * rsize
    west = lax.rem(gx + nx - 1, nx)
    east = lax.rem(gx + 1, nx)
    south = lax.rem(gy + lanes - 1, lanes)
    north = lax.rem(gy + 1, lanes)

    def send(src, dst, ssem, rsem, to):
        copy = pltpu.make_async_remote_copy(
            src_ref=src, dst_ref=dst, send_sem=ssem, recv_sem=rsem,
            device_id=to, device_id_type=MESH,
        )
        copy.start()
        return copy

    partners = []
    for d in range(1, rsize):
        partners.append((gx, line0 + lax.rem(place + d, rsize)))
    for d in range(1, rows_n):
        partners.append((gx, lax.rem(line + d, rows_n) * rsize + place))
    for d in range(rsize):
        mate = line0 + lax.rem(place + d, rsize)
        partners.append((west, mate))
        partners.append((east, mate))
    partners += [(gx, south), (gx, north), (west, south), (east, north)]
    barrier = pltpu.get_barrier_semaphore()
    for to in partners:
        pl.semaphore_signal(barrier, inc=1, device_id=to, device_id_type=MESH)

    for c in range(comps):
        edge[c : c + 1, :] = vel[c, last : last + 1, :]
        edge[3 + c : 4 + c, :] = vel[c, 0:1, :]
    edge[6:8, :] = jnp.zeros((2, cz), F32)
    for n, value in enumerate((piv[0, last], bwd[0, last], piv[1, last], bwd[1, last])):
        edge[6:7, n * 128 : (n + 1) * 128] = jnp.full((1, 128), value, F32)

    pl.semaphore_wait(barrier, len(partners))

    pending = []

    def send_planes(k, src):
        a = send(src, planes.at[k, 1], pls.at[k, 0], plr.at[k, 0], (west, gy))
        b = send(src, planes.at[k, 0], pls.at[k, 1], plr.at[k, 1], (east, gy))
        pending.extend([a, b])
        return a, b

    plane_copies = send_planes(0, vel)
    edge_copies = [
        send(edge, edge_in.at[0], eds.at[0], edr.at[0], (gx, north)),
        send(edge, edge_in.at[1], eds.at[1], edr.at[1], (gx, south)),
        send(edge, edge_in.at[2], eds.at[2], edr.at[2], (west, south)),
    ]
    pending.extend(edge_copies)

    row16 = lax.broadcasted_iota(jnp.int32, (cy, chunk), 0)
    lane = lax.broadcasted_iota(jnp.int32, (1, chunk), 1)
    zblock = min(256, cz)
    zrow = lax.broadcasted_iota(jnp.int32, (zblock, chunk), 0)
    c0, c1, c2 = count[0], count[1], count[2]
    speed[...] = jnp.zeros_like(speed)
    fluid[...] = jnp.zeros_like(fluid)

    def prepare(i, _):
        at = pl.ds(pl.multiple_of(i * chunk, chunk), chunk)
        where = cell[:, at]
        zpos = lax.rem(where, cz)
        ypos = lax.rem(lax.div(where, cz), cy)
        for n in range(cz // zblock):
            onehot[n * zblock : (n + 1) * zblock, at] = jnp.where(
                zrow + n * zblock == zpos, 1.0, 0.0
            ).astype(BF16)
        ox, oy, oz = offset[0:1, at], offset[1:2, at], offset[2:3, at]
        here = row16 == ypos
        above = row16 == ypos + 1
        ymask[:, at] = jnp.where(here, 1.0, 0.0)
        ywt[:, at] = jnp.where(here, 1.0 - oy, jnp.where(above, oy, 0.0))
        wts[0:1, at] = (1.0 - ox) * (1.0 - oz)
        wts[1:2, at] = (1.0 - ox) * oz
        wts[2:3, at] = ox * (1.0 - oz)
        wts[3:4, at] = ox * oz
        wts[4:5, at] = jnp.where(ypos == last, oy, 0.0)
        slot = lane + i * chunk
        out = slot - RESIDENT
        turn = jnp.where(out < CAP, out, jnp.where(out < 2 * CAP, out - CAP, out - 2 * CAP))
        limit = jnp.where(out < CAP, c0, jnp.where(out < 2 * CAP, c1, c2))
        live_ref[:, at] = jnp.where((out < 0) | (turn < limit), 1.0, 0.0)
        speed[0:3, at] = pvel[:, at]
        return 0

    lax.fori_loop(0, steps, prepare, 0)

    lane128 = lax.broadcasted_iota(jnp.int32, (1, 128), 1)
    for k in range(SECTIONS):
        g = jnp.zeros((1, 128), F32)
        gs = []
        for j in range(cy):
            g = jnp.where(lane128 == j, 1.0, 0.0) + fwd[k, j] * g
            gs.append(g)
        u = jnp.zeros((1, 128), F32)
        for j in reversed(range(cy)):
            u = piv[k, j] * gs[j] + bwd[k, j] * u
            unit_rows[j : j + 1, :] = u
        block = unit_rows[...]
        for i in range(cy):
            solve_cols[k, i] = jnp.broadcast_to(block[:, i : i + 1], (cy, 128))
        alpha[k] = jnp.broadcast_to(block[:, 0:1] * fwd[k, 0], (cy, cz))
        weight = jnp.float32(1.0)
        shrink = jnp.float32(1.0)
        for j in reversed(range(cy)):
            carry_col[k, j : j + 1, :] = jnp.full((1, 128), weight, F32)
            weight = weight * fwd[k, j]
            shrink = shrink * bwd[k, j]
            beta[k, j : j + 1, :] = jnp.full((1, cz), shrink, F32)
        for t in range(rsize):
            msg[k, t, 6:7, :] = jnp.full((1, width), weight, F32)
            half = lax.broadcasted_iota(jnp.int32, (1, width), 1) < width // 2
            msg[k, t, 7:8, :] = jnp.where(half, alpha[k, 0:1, 0:width], shrink)
    for j in range(cy):
        ymet[j : j + 1, :] = jnp.full((1, cz), 0.5 * metric[j], F32)

    def responses(i, _):
        at = pl.ds(pl.multiple_of(i * chunk, chunk), chunk)
        top = wts[4:5, at]
        w = ywt[:, at]
        zero = jnp.zeros((3, chunk), F32)
        two = jnp.zeros((2, chunk), F32)
        ab[0, :, at] = jnp.concatenate([zero, top, top, top, two], axis=0)
        for k in range(1, SECTIONS):
            a = jnp.sum(w * alpha[k - 1, :, 0:1], axis=0, keepdims=True)
            b = jnp.sum(w * beta[k - 1, :, 0:1], axis=0, keepdims=True) + top
            ab[k, :, at] = jnp.concatenate([a, a, a, b, b, b, two], axis=0)
        return 0

    lax.fori_loop(0, steps, responses, 0)

    def gather_plane(source, side):
        for c in range(comps):
            x = source[c]
            high, low = halves(x)
            table[0, c * cy : (c + 1) * cy, :] = high
            table[1, c * cy : (c + 1) * cy, :] = low
            high, low = halves(pltpu.roll(x, cz - 1, 1))
            at = (comps + c) * cy
            table[0, at : at + cy, :] = high
            table[1, at : at + cy, :] = low

        def one(i, _):
            at = pl.ds(pl.multiple_of(i * chunk, chunk), chunk)
            hot = onehot[:, at]
            got = jnp.dot(table[0], hot, preferred_element_type=F32) + jnp.dot(
                table[1], hot, preferred_element_type=F32
            )
            w0 = wts[2 * side : 2 * side + 1, at]
            w1 = wts[2 * side + 1 : 2 * side + 2, at]
            w = ywt[:, at]
            rows = []
            for c in range(comps):
                near = got[c * cy : (c + 1) * cy]
                far = got[(comps + c) * cy : (comps + c + 1) * cy]
                rows.append(jnp.sum((w0 * near + w1 * far) * w, axis=0, keepdims=True))
            value = jnp.concatenate(rows, axis=0)
            if side == 0:
                fluid[0:3, at] = value
            else:
                fluid[0:3, at] = fluid[0:3, at] + value
            return 0

        lax.fori_loop(0, steps, one, 0)

    sub = lax.broadcasted_iota(jnp.int32, (8, width), 0)
    col = lax.broadcasted_iota(jnp.int32, (8, width), 1)

    def coefficients(x):
        grow = jnp.broadcast_to(x[6:7], (8, width))
        seven = jnp.broadcast_to(x[7:8], (8, width))
        other = pltpu.roll(seven, width // 2, 1)
        mixed = jnp.where(col < width // 2, seven, other)
        shrink = jnp.where(col < width // 2, other, seven)
        return grow, mixed, shrink

    def lifted(e):
        return jnp.where((sub >= 3) & (sub < 6), pltpu.roll(e, 3, 0), jnp.where(sub == 6, e, 0.0))

    def down(x, grow, e):
        return jnp.where(sub < 3, x, 0.0) + grow * e

    def up(x, mixed, shrink, e, l):
        return jnp.where((sub >= 3) & (sub < 6), x, 0.0) + mixed * lifted(e) + shrink * l

    def plane_rows(k, slot):
        return jnp.concatenate([el[k, slot, t] for t in range(rsize)], axis=1)

    below_edge = jnp.where(gy > 0, 1.0, 0.0).astype(F32)
    above_edge = jnp.where(gy < lanes - 1, 1.0, 0.0).astype(F32)

    gather_plane(vel, 0)
    for copy in edge_copies:
        copy.wait_recv()
    for copy in plane_copies:
        copy.wait_recv()
    gather_plane(planes.at[0, 1], 1)

    for k in range(SECTIONS):
        step = TIME_STEP * SECTION_WEIGHTS[k]
        if k == 0:
            sub_full = lax.broadcasted_iota(jnp.int32, (8, cz), 0)
            upper = jnp.where((sub_full >= 3) & (sub_full < 6), 1.0, 0.0) * above_edge
            lower = jnp.where(sub_full < 3, 1.0, 0.0) * below_edge
            own = edge_in[0] * lower + edge_in[1] * upper
            plus = edge_in[2] * upper
            minus = None
        else:
            own, minus, plus = plane_rows(k - 1, 0), plane_rows(k - 1, 1), plane_rows(k - 1, 2)
        pair = jnp.concatenate([own, plus], axis=0)
        high, low = halves(pair)
        el_table[0, 0:16, :] = high
        el_table[1, 0:16, :] = low
        high, low = halves(pltpu.roll(pair, cz - 1, 1))
        el_table[0, 16:32, :] = high
        el_table[1, 16:32, :] = low

        def push(i, _, k=k, step=step):
            at = pl.ds(pl.multiple_of(i * chunk, chunk), chunk)
            hot = onehot[:, at]
            got = jnp.dot(el_table[0], hot, preferred_element_type=F32) + jnp.dot(
                el_table[1], hot, preferred_element_type=F32
            )
            mix = (
                wts[0:1, at] * got[0:8]
                + wts[2:3, at] * got[8:16]
                + wts[1:2, at] * got[16:24]
                + wts[3:4, at] * got[24:32]
            ) * ab[k, :, at]
            flow = fluid[:, at] + mix + pltpu.roll(mix, 5, 0)
            now = speed[:, at]
            drag = tau[:, at] * (flow - now)
            speed[:, at] = now + step * drag
            share = drag * (-COUPLING * live_ref[:, at])
            mask = ymask[:, at]
            for c in range(comps):
                one = share[c : c + 1]
                head = one.astype(BF16).astype(F32)
                scat[c * cy : (c + 1) * cy, at] = (mask * head).astype(BF16)
                scat[(comps + c) * cy : (comps + c + 1) * cy, at] = (mask * (one - head)).astype(BF16)
            return 0

        lax.fori_loop(0, steps, push, 0)

        if k == SECTIONS - 1:
            moved[...] = speed[...] * live_ref[...]
            trips = [
                send(moved.at[:, RESIDENT : RESIDENT + CAP], mig.at[0], mgs.at[0], mgr.at[0], (east, gy)),
                send(moved.at[:, RESIDENT + CAP : RESIDENT + 2 * CAP], mig.at[1], mgs.at[1], mgr.at[1], (gx, south)),
                send(moved.at[:, RESIDENT + 2 * CAP : RESIDENT + 3 * CAP], mig.at[2], mgs.at[2], mgr.at[2], (gx, north)),
            ]
            pending.extend(trips)

        def gathered(n, _):
            at = pl.ds(pl.multiple_of(n * zblock, zblock), zblock)
            both = lax.dot_general(
                scat[...], onehot[at, :], (((1,), (1,)), ((), ())), preferred_element_type=F32
            )
            half = comps * cy
            accum[:, at] = both[0:half] + both[half : 2 * half]
            return 0

        lax.fori_loop(0, cz // zblock, gathered, 0)

        def plane(source, c, rows):
            if k == 0:
                return source[c]
            return source[c] + alpha[k - 1] * rows[c : c + 1] + beta[k - 1] * rows[3 + c : 4 + c]

        for c in range(comps):
            uref[c] = plane(vel if k == 0 else part.at[k - 1], c, own)
        rowz = lax.broadcasted_iota(jnp.int32, (cy, cz), 0)
        for c in range(comps):
            u = uref[c]
            slope_x = (plane(planes.at[k, 1], c, plus) - plane(planes.at[k, 0], c, minus)) * (
                0.5 * STREAM_SCALE
            )
            slope_z = (pltpu.roll(u, cz - 1, 1) - pltpu.roll(u, 1, 1)) * (0.5 * SPAN_SCALE)
            if k == 0:
                under = own[c : c + 1]
            else:
                rate = edge_in[0, 6:7, :]
                base = 256 * (k - 1)
                pv = jnp.concatenate([rate[:, base : base + 128]] * (cz // 128), axis=1)
                bv = jnp.concatenate([rate[:, base + 128 : base + 256]] * (cz // 128), axis=1)
                under = (pv * own[c : c + 1] + bv * u[0:1]) * below_edge
            upper_y = jnp.where(rowz == last, own[3 + c : 4 + c], pltpu.roll(u, cy - 1, 0))
            lower_y = jnp.where(rowz == 0, under, pltpu.roll(u, 1, 0))
            slope_y = (upper_y - lower_y) * ymet[...]
            convection = -(uref[0] * slope_x + uref[1] * slope_y + uref[2] * slope_z)
            rhs_ref[c] = u + step * (convection + accum[c * cy : (c + 1) * cy, :])

        for c in range(comps):
            for z in range(cz // 128):
                at = slice(z * 128, (z + 1) * 128)
                total = None
                for i in range(cy):
                    term = solve_cols[k, i] * rhs_ref[c, i : i + 1, at]
                    total = term if total is None else total + term
                part[k, c, :, at] = total
                leave = jnp.sum(carry_col[k] * rhs_ref[c, :, at], axis=0, keepdims=True)
                t, o = (z * 128) // width, (z * 128) % width
                msg[k, t, c : c + 1, o : o + 128] = leave
                msg[k, t, 3 + c : 4 + c, o : o + 128] = total[0:1]

        first = []
        for d in range(1, rsize):
            to = lax.rem(place + d, rsize)
            first.append(
                send(msg.at[k, to], got1.at[k, place], s1s.at[k, d - 1], s1r.at[k, d - 1], (gx, line0 + to))
            )
        pending.extend(first)
        got1[k, place] = msg[k, place]
        if k < SECTIONS - 1:
            plane_copies = send_planes(k + 1, part.at[k])
            gather_plane(part.at[k], 0)
        for copy in first:
            copy.wait_recv()
        tiles = [got1[k, t] for t in range(rsize)]
        coefs = [coefficients(x) for x in tiles]
        e = jnp.where(sub == 6, 1.0, 0.0)
        starts = []
        for t in range(rsize):
            starts.append(e)
            e = down(tiles[t], coefs[t][0], e)
        l = jnp.where(sub == 7, 1.0, 0.0)
        for t in reversed(range(rsize)):
            l = up(tiles[t], coefs[t][1], coefs[t][2], starts[t], l)
        whole = jnp.where(
            (sub < 3) | (sub == 6),
            e,
            jnp.where((sub == 7) & (col < width // 2), pltpu.roll(l, 1, 0), l),
        )
        own2[k] = whole
        got2[k, line] = whole
        second = []
        for d in range(1, rows_n):
            to = lax.rem(line + d, rows_n)
            second.append(
                send(own2.at[k], got2.at[k, line], s2s.at[k, d - 1], s2r.at[k, d - 1], (gx, to * rsize + place))
            )
        pending.extend(second)
        for copy in second:
            copy.wait_recv()
        maps = [got2[k, q] for q in range(rows_n)]
        mcoefs = [coefficients(x) for x in maps]
        e = jnp.zeros((8, width), F32)
        e_row = jnp.zeros((8, width), F32)
        starts = []
        for q in range(rows_n):
            starts.append(e)
            e_row = jnp.where(line == q, e, e_row)
            e = down(maps[q], mcoefs[q][0], e)
        l = jnp.zeros((8, width), F32)
        l_row = jnp.zeros((8, width), F32)
        for q in reversed(range(rows_n)):
            l_row = jnp.where(line == q, l, l_row)
            l = up(maps[q], mcoefs[q][1], mcoefs[q][2], starts[q], l)
        e = jnp.where(sub < 3, e_row, 0.0)
        starts = []
        for t in range(rsize):
            starts.append(e)
            e = down(tiles[t], coefs[t][0], e)
        l = l_row
        for t in reversed(range(rsize)):
            ans[k, t] = jnp.where(sub < 3, starts[t], jnp.where(sub < 6, l, 0.0))
            l = up(tiles[t], coefs[t][1], coefs[t][2], starts[t], l)
        third = []
        for d in range(rsize):
            to = lax.rem(place + d, rsize)
            mate = line0 + to
            if d > 0:
                third.append(
                    send(ans.at[k, to], el.at[k, 0, place], s3s.at[k, 0, d], s3r.at[k, 0, d], (gx, mate))
                )
            if k < SECTIONS - 1:
                third.append(
                    send(ans.at[k, to], el.at[k, 1, place], s3s.at[k, 1, d], s3r.at[k, 1, d], (east, mate))
                )
                third.append(
                    send(ans.at[k, to], el.at[k, 2, place], s3s.at[k, 2, d], s3r.at[k, 2, d], (west, mate))
                )
        pending.extend(third)
        el[k, 0, place] = ans[k, place]
        if k < SECTIONS - 1:
            for copy in plane_copies:
                copy.wait_recv()
            gather_plane(planes.at[k + 1, 1], 1)
        else:
            for copy in trips:
                copy.wait_recv()
            part_out[:, 0:RESIDENT] = moved[0:3, 0:RESIDENT]
            part_out[:, RESIDENT : RESIDENT + CAP] = mig[0, 0:3, :]
            part_out[:, RESIDENT + CAP : RESIDENT + 2 * CAP] = mig[1, 0:3, :] * above_edge
            part_out[:, RESIDENT + 2 * CAP : RESIDENT + 3 * CAP] = mig[2, 0:3, :] * below_edge
        for copy in third:
            copy.wait_recv()

    rows = plane_rows(SECTIONS - 1, 0)
    k = SECTIONS - 1
    for c in range(comps):
        field_out[c] = part[k, c] + alpha[k] * rows[c : c + 1] + beta[k] * rows[3 + c : 4 + c]
    for copy in pending:
        copy.wait_send()


def on_device(
    velocity, y_metric, forward_rate, backward_rate, pivot_inv,
    particle_vel, particle_cell, particle_offset, inverse_tau, outgoing_count,
):
    comps, _, cy, cz = velocity.shape
    slots = particle_vel.shape[1]
    nx, lanes = lax.axis_size("gx"), lax.axis_size("gy")
    rsize = row_size(lanes)
    rows_n = lanes // rsize
    width = cz // rsize
    vmem, smem = pltpu.VMEM, pl.BlockSpec(memory_space=pltpu.SMEM)
    whole = pl.BlockSpec(memory_space=pltpu.VMEM)
    dma = pltpu.SemaphoreType.DMA
    scratch = [
        vmem((cz, slots), BF16),
        vmem((2, 2 * comps * cy, cz), BF16),
        vmem((2, 32, cz), BF16),
        vmem((2 * comps * cy, slots), BF16),
        vmem((comps * cy, cz), F32),
        vmem((8, slots), F32),
        vmem((cy, slots), F32),
        vmem((cy, slots), F32),
        vmem((SECTIONS, 8, slots), F32),
        vmem((8, slots), F32),
        vmem((8, slots), F32),
        vmem((1, slots), F32),
        vmem((8, slots), F32),
        vmem((SECTIONS, cy, cy, 128), F32),
        vmem((SECTIONS, cy, 128), F32),
        vmem((SECTIONS, cy, cz), F32),
        vmem((SECTIONS, cy, cz), F32),
        vmem((cy, cz), F32),
        vmem((cy, 128), F32),
        vmem((SECTIONS, comps, cy, cz), F32),
        vmem((SECTIONS, 2, comps, cy, cz), F32),
        vmem((comps, cy, cz), F32),
        vmem((comps, cy, cz), F32),
        vmem((8, cz), F32),
        vmem((3, 8, cz), F32),
        vmem((SECTIONS, rsize, 8, width), F32),
        vmem((SECTIONS, rsize, 8, width), F32),
        vmem((SECTIONS, rows_n, 8, width), F32),
        vmem((SECTIONS, 8, width), F32),
        vmem((SECTIONS, rsize, 8, width), F32),
        vmem((SECTIONS, 3, rsize, 8, width), F32),
        vmem((3, 8, CAP), F32),
        dma((SECTIONS, rsize - 1)), dma((SECTIONS, rsize - 1)),
        dma((SECTIONS, rows_n - 1)), dma((SECTIONS, rows_n - 1)),
        dma((SECTIONS, 3, rsize)), dma((SECTIONS, 3, rsize)),
        dma((SECTIONS, 2)), dma((SECTIONS, 2)),
        dma((3,)), dma((3,)), dma((3,)), dma((3,)),
    ]
    field, moved = pl.pallas_call(
        functools.partial(kernel, (nx, lanes, rsize)),
        out_shape=(
            jax.ShapeDtypeStruct((comps, cy, cz), F32),
            jax.ShapeDtypeStruct((comps, slots), F32),
        ),
        in_specs=[whole, smem, smem, smem, smem, whole, whole, whole, whole, smem],
        out_specs=(whole, whole),
        scratch_shapes=scratch,
        compiler_params=pltpu.CompilerParams(
            collective_id=0, has_side_effects=True, vmem_limit_bytes=48 * 1024 * 1024
        ),
        name="channel_sections",
    )(
        velocity.reshape(comps, cy, cz),
        y_metric,
        forward_rate,
        backward_rate,
        pivot_inv,
        particle_vel,
        particle_cell.reshape(1, slots),
        particle_offset,
        inverse_tau.reshape(1, slots),
        outgoing_count.reshape(3),
    )
    return field.reshape(velocity.shape), moved


def solution(mesh):
    return jax.shard_map(
        on_device,
        mesh=mesh,
        in_specs=(
            P(None, "gx", "gy", None),
            P("gy"),
            P(None, "gy"),
            P(None, "gy"),
            P(None, "gy"),
            P(None, ("gx", "gy")),
            P(("gx", "gy")),
            P(None, ("gx", "gy")),
            P(("gx", "gy")),
            P("gx", "gy", None),
        ),
        out_specs=(P(None, "gx", "gy", None), P(None, ("gx", "gy"))),
        check_vma=False,
    )
```

```python
import functools

import jax
import jax.numpy as jnp
from jax import lax
from jax.experimental import pallas as pl
from jax.experimental.pallas import tpu as pltpu
from jax.sharding import PartitionSpec as P

RESIDENT = 2048
CAP = 512
SECTIONS = 3
SECTION_WEIGHTS = (8.0 / 15.0, 5.0 / 12.0, 3.0 / 4.0)
TIME_STEP = 0.3
STREAM_SCALE = 2.0
SPAN_SCALE = 2.0
COUPLING = 0.5
CHUNK = 512
MESH = pl.DeviceIdType.MESH
F32 = jnp.float32
BF16 = jnp.bfloat16


def row_size(lanes):
    return 8 if lanes == 32 else max(2, lanes // 2)


def halves(x):
    high = x.astype(BF16)
    return high, (x - high.astype(F32)).astype(BF16)


def kernel(
    dims,
    vel, metric, fwd, bwd, piv, pvel, cell, offset, tau, count,
    field_out, part_out,
    onehot, table, el_table, scat, accum, wts, ymask, ywt, ab, speed, fluid, live_ref, moved,
    solve_cols, carry_col, alpha, beta, ymet, unit_rows,
    part, planes, uref, rhs_ref, edge, edge_in, msg, got1, got2, own2, ans, el, mig,
    s1s, s1r, s2s, s2r, s3s, s3r, pls, plr, eds, edr, mgs, mgr,
):
    nx, lanes, rsize = dims
    rows_n = lanes // rsize
    comps, cy, cz = vel.shape
    width = cz // rsize
    slots = pvel.shape[1]
    chunk = min(CHUNK, slots)
    steps = slots // chunk
    last = cy - 1
    rows6 = 2 * comps * cy
    gx = lax.axis_index("gx")
    gy = lax.axis_index("gy")
    place = lax.rem(gy, rsize)
    line = gy // rsize
    line0 = line * rsize
    west = lax.rem(gx + nx - 1, nx)
    east = lax.rem(gx + 1, nx)
    south = lax.rem(gy + lanes - 1, lanes)
    north = lax.rem(gy + 1, lanes)

    def send(src, dst, ssem, rsem, to):
        copy = pltpu.make_async_remote_copy(
            src_ref=src, dst_ref=dst, send_sem=ssem, recv_sem=rsem,
            device_id=to, device_id_type=MESH,
        )
        copy.start()
        return copy

    partners = []
    for d in range(1, rsize):
        partners.append((gx, line0 + lax.rem(place + d, rsize)))
    for d in range(1, rows_n):
        partners.append((gx, lax.rem(line + d, rows_n) * rsize + place))
    for d in range(rsize):
        mate = line0 + lax.rem(place + d, rsize)
        partners.append((west, mate))
        partners.append((east, mate))
    partners += [(gx, south), (gx, north), (west, south), (east, north)]
    barrier = pltpu.get_barrier_semaphore()
    for to in partners:
        pl.semaphore_signal(barrier, inc=1, device_id=to, device_id_type=MESH)

    for c in range(comps):
        edge[c : c + 1, :] = vel[c, last : last + 1, :]
        edge[3 + c : 4 + c, :] = vel[c, 0:1, :]
    edge[6:8, :] = jnp.zeros((2, cz), F32)
    for n, value in enumerate((piv[0, last], bwd[0, last], piv[1, last], bwd[1, last])):
        edge[6:7, n * 128 : (n + 1) * 128] = jnp.full((1, 128), value, F32)

    pl.semaphore_wait(barrier, len(partners))

    pending = []

    def send_planes(k, src):
        a = send(src, planes.at[k, 1], pls.at[k, 0], plr.at[k, 0], (west, gy))
        b = send(src, planes.at[k, 0], pls.at[k, 1], plr.at[k, 1], (east, gy))
        pending.extend([a, b])
        return a, b

    plane_copies = send_planes(0, vel)
    edge_copies = [
        send(edge, edge_in.at[0], eds.at[0], edr.at[0], (gx, north)),
        send(edge, edge_in.at[1], eds.at[1], edr.at[1], (gx, south)),
        send(edge, edge_in.at[2], eds.at[2], edr.at[2], (west, south)),
    ]
    pending.extend(edge_copies)

    row16 = lax.broadcasted_iota(jnp.int32, (cy, chunk), 0)
    lane = lax.broadcasted_iota(jnp.int32, (1, chunk), 1)
    zblock = min(256, cz)
    zrow = lax.broadcasted_iota(jnp.int32, (zblock, chunk), 0)
    c0, c1, c2 = count[0], count[1], count[2]
    speed[...] = jnp.zeros_like(speed)
    fluid[...] = jnp.zeros_like(fluid)

    def prepare(i, _):
        at = pl.ds(pl.multiple_of(i * chunk, chunk), chunk)
        where = cell[:, at]
        zpos = lax.rem(where, cz)
        ypos = lax.rem(lax.div(where, cz), cy)
        for n in range(cz // zblock):
            onehot[n * zblock : (n + 1) * zblock, at] = jnp.where(
                zrow + n * zblock == zpos, 1.0, 0.0
            ).astype(BF16)
        ox, oy, oz = offset[0:1, at], offset[1:2, at], offset[2:3, at]
        here = row16 == ypos
        above = row16 == ypos + 1
        ymask[:, at] = jnp.where(here, 1.0, 0.0)
        ywt[:, at] = jnp.where(here, 1.0 - oy, jnp.where(above, oy, 0.0))
        wts[0:1, at] = (1.0 - ox) * (1.0 - oz)
        wts[1:2, at] = (1.0 - ox) * oz
        wts[2:3, at] = ox * (1.0 - oz)
        wts[3:4, at] = ox * oz
        wts[4:5, at] = jnp.where(ypos == last, oy, 0.0)
        slot = lane + i * chunk
        out = slot - RESIDENT
        turn = jnp.where(out < CAP, out, jnp.where(out < 2 * CAP, out - CAP, out - 2 * CAP))
        limit = jnp.where(out < CAP, c0, jnp.where(out < 2 * CAP, c1, c2))
        live_ref[:, at] = jnp.where((out < 0) | (turn < limit), 1.0, 0.0)
        speed[0:3, at] = pvel[:, at]
        return 0

    lax.fori_loop(0, steps, prepare, 0)

    lane128 = lax.broadcasted_iota(jnp.int32, (1, 128), 1)
    for k in range(SECTIONS):
        g = jnp.zeros((1, 128), F32)
        gs = []
        for j in range(cy):
            g = jnp.where(lane128 == j, 1.0, 0.0) + fwd[k, j] * g
            gs.append(g)
        u = jnp.zeros((1, 128), F32)
        for j in reversed(range(cy)):
            u = piv[k, j] * gs[j] + bwd[k, j] * u
            unit_rows[j : j + 1, :] = u
        block = unit_rows[...]
        for i in range(cy):
            solve_cols[k, i] = jnp.broadcast_to(block[:, i : i + 1], (cy, 128))
        alpha[k] = jnp.broadcast_to(block[:, 0:1] * fwd[k, 0], (cy, cz))
        weight = jnp.float32(1.0)
        shrink = jnp.float32(1.0)
        for j in reversed(range(cy)):
            carry_col[k, j : j + 1, :] = jnp.full((1, 128), weight, F32)
            weight = weight * fwd[k, j]
            shrink = shrink * bwd[k, j]
            beta[k, j : j + 1, :] = jnp.full((1, cz), shrink, F32)
        for t in range(rsize):
            msg[k, t, 6:7, :] = jnp.full((1, width), weight, F32)
            half = lax.broadcasted_iota(jnp.int32, (1, width), 1) < width // 2
            msg[k, t, 7:8, :] = jnp.where(half, alpha[k, 0:1, 0:width], shrink)
    for j in range(cy):
        ymet[j : j + 1, :] = jnp.full((1, cz), 0.5 * metric[j], F32)

    def responses(i, _):
        at = pl.ds(pl.multiple_of(i * chunk, chunk), chunk)
        top = wts[4:5, at]
        w = ywt[:, at]
        zero = jnp.zeros((3, chunk), F32)
        two = jnp.zeros((2, chunk), F32)
        ab[0, :, at] = jnp.concatenate([zero, top, top, top, two], axis=0)
        for k in range(1, SECTIONS):
            a = jnp.sum(w * alpha[k - 1, :, 0:1], axis=0, keepdims=True)
            b = jnp.sum(w * beta[k - 1, :, 0:1], axis=0, keepdims=True) + top
            ab[k, :, at] = jnp.concatenate([a, a, a, b, b, b, two], axis=0)
        return 0

    lax.fori_loop(0, steps, responses, 0)

    def gather_plane(source, side):
        for c in range(comps):
            x = source[c]
            high, low = halves(x)
            table[c * cy : (c + 1) * cy, :] = high
            table[rows6 + c * cy : rows6 + (c + 1) * cy, :] = low
            high, low = halves(pltpu.roll(x, cz - 1, 1))
            at = (comps + c) * cy
            table[at : at + cy, :] = high
            table[rows6 + at : rows6 + at + cy, :] = low

        def one(i):
            at = slice(i * chunk, (i + 1) * chunk)
            hot = onehot[:, at]
            got = jnp.dot(table[...], hot, preferred_element_type=F32)
            got = got[0:rows6] + got[rows6 : 2 * rows6]
            w0 = wts[2 * side : 2 * side + 1, at]
            w1 = wts[2 * side + 1 : 2 * side + 2, at]
            w = ywt[:, at]
            rows = []
            for c in range(comps):
                near = got[c * cy : (c + 1) * cy]
                far = got[(comps + c) * cy : (comps + c + 1) * cy]
                rows.append(jnp.sum((w0 * near + w1 * far) * w, axis=0, keepdims=True))
            value = jnp.concatenate(rows, axis=0)
            if side == 0:
                fluid[0:3, at] = value
            else:
                fluid[0:3, at] = fluid[0:3, at] + value

        for i in range(steps):
            one(i)

    sub = lax.broadcasted_iota(jnp.int32, (8, width), 0)
    col = lax.broadcasted_iota(jnp.int32, (8, width), 1)

    def coefficients(x):
        grow = jnp.broadcast_to(x[6:7], (8, width))
        seven = jnp.broadcast_to(x[7:8], (8, width))
        other = pltpu.roll(seven, width // 2, 1)
        mixed = jnp.where(col < width // 2, seven, other)
        shrink = jnp.where(col < width // 2, other, seven)
        return grow, mixed, shrink

    def lifted(e):
        return jnp.where((sub >= 3) & (sub < 6), pltpu.roll(e, 3, 0), jnp.where(sub == 6, e, 0.0))

    def down(x, grow, e):
        return jnp.where(sub < 3, x, 0.0) + grow * e

    def up(x, mixed, shrink, e, l):
        return jnp.where((sub >= 3) & (sub < 6), x, 0.0) + mixed * lifted(e) + shrink * l

    def plane_rows(k, slot):
        return jnp.concatenate([el[k, slot, t] for t in range(rsize)], axis=1)

    below_edge = jnp.where(gy > 0, 1.0, 0.0).astype(F32)
    above_edge = jnp.where(gy < lanes - 1, 1.0, 0.0).astype(F32)

    gather_plane(vel, 0)
    for copy in edge_copies:
        copy.wait_recv()
    for copy in plane_copies:
        copy.wait_recv()
    gather_plane(planes.at[0, 1], 1)

    for k in range(SECTIONS):
        step = TIME_STEP * SECTION_WEIGHTS[k]
        if k == 0:
            sub_full = lax.broadcasted_iota(jnp.int32, (8, cz), 0)
            upper = jnp.where((sub_full >= 3) & (sub_full < 6), 1.0, 0.0) * above_edge
            lower = jnp.where(sub_full < 3, 1.0, 0.0) * below_edge
            own = edge_in[0] * lower + edge_in[1] * upper
            plus = edge_in[2] * upper
            minus = None
        else:
            own, minus, plus = plane_rows(k - 1, 0), plane_rows(k - 1, 1), plane_rows(k - 1, 2)
        pair = jnp.concatenate([own, plus], axis=0)
        high, low = halves(pair)
        el_table[0:16, :] = high
        el_table[32:48, :] = low
        high, low = halves(pltpu.roll(pair, cz - 1, 1))
        el_table[16:32, :] = high
        el_table[48:64, :] = low

        def push(i, k=k, step=step):
            at = slice(i * chunk, (i + 1) * chunk)
            hot = onehot[:, at]
            got = jnp.dot(el_table[...], hot, preferred_element_type=F32)
            got = got[0:32] + got[32:64]
            mix = (
                wts[0:1, at] * got[0:8]
                + wts[2:3, at] * got[8:16]
                + wts[1:2, at] * got[16:24]
                + wts[3:4, at] * got[24:32]
            ) * ab[k, :, at]
            flow = fluid[:, at] + mix + pltpu.roll(mix, 5, 0)
            now = speed[:, at]
            drag = tau[:, at] * (flow - now)
            speed[:, at] = now + step * drag
            share = drag * (-COUPLING * live_ref[:, at])
            mask = ymask[:, at]
            for c in range(comps):
                one = share[c : c + 1]
                head = one.astype(BF16).astype(F32)
                scat[c * cy : (c + 1) * cy, at] = (mask * head).astype(BF16)
                scat[(comps + c) * cy : (comps + c + 1) * cy, at] = (mask * (one - head)).astype(BF16)

        for i in range(steps):
            push(i)

        if k == SECTIONS - 1:
            moved[...] = speed[...] * live_ref[...]
            trips = [
                send(moved.at[:, RESIDENT : RESIDENT + CAP], mig.at[0], mgs.at[0], mgr.at[0], (east, gy)),
                send(moved.at[:, RESIDENT + CAP : RESIDENT + 2 * CAP], mig.at[1], mgs.at[1], mgr.at[1], (gx, south)),
                send(moved.at[:, RESIDENT + 2 * CAP : RESIDENT + 3 * CAP], mig.at[2], mgs.at[2], mgr.at[2], (gx, north)),
            ]
            pending.extend(trips)

        def gathered(n):
            at = slice(n * zblock, (n + 1) * zblock)
            both = lax.dot_general(
                scat[...], onehot[at, :], (((1,), (1,)), ((), ())), preferred_element_type=F32
            )
            half = comps * cy
            accum[:, at] = both[0:half] + both[half : 2 * half]

        for n in range(cz // zblock):
            gathered(n)

        def plane(source, c, rows):
            if k == 0:
                return source[c]
            return source[c] + alpha[k - 1] * rows[c : c + 1] + beta[k - 1] * rows[3 + c : 4 + c]

        for c in range(comps):
            uref[c] = plane(vel if k == 0 else part.at[k - 1], c, own)
        rowz = lax.broadcasted_iota(jnp.int32, (cy, cz), 0)
        for c in range(comps):
            u = uref[c]
            slope_x = (plane(planes.at[k, 1], c, plus) - plane(planes.at[k, 0], c, minus)) * (
                0.5 * STREAM_SCALE
            )
            slope_z = (pltpu.roll(u, cz - 1, 1) - pltpu.roll(u, 1, 1)) * (0.5 * SPAN_SCALE)
            if k == 0:
                under = own[c : c + 1]
            else:
                rate = edge_in[0, 6:7, :]
                base = 256 * (k - 1)
                pv = jnp.concatenate([rate[:, base : base + 128]] * (cz // 128), axis=1)
                bv = jnp.concatenate([rate[:, base + 128 : base + 256]] * (cz // 128), axis=1)
                under = (pv * own[c : c + 1] + bv * u[0:1]) * below_edge
            upper_y = jnp.where(rowz == last, own[3 + c : 4 + c], pltpu.roll(u, cy - 1, 0))
            lower_y = jnp.where(rowz == 0, under, pltpu.roll(u, 1, 0))
            slope_y = (upper_y - lower_y) * ymet[...]
            convection = -(uref[0] * slope_x + uref[1] * slope_y + uref[2] * slope_z)
            rhs_ref[c] = u + step * (convection + accum[c * cy : (c + 1) * cy, :])

        for c in range(comps):
            for z in range(cz // 128):
                at = slice(z * 128, (z + 1) * 128)
                total = None
                for i in range(cy):
                    term = solve_cols[k, i] * rhs_ref[c, i : i + 1, at]
                    total = term if total is None else total + term
                part[k, c, :, at] = total
                leave = jnp.sum(carry_col[k] * rhs_ref[c, :, at], axis=0, keepdims=True)
                t, o = (z * 128) // width, (z * 128) % width
                msg[k, t, c : c + 1, o : o + 128] = leave
                msg[k, t, 3 + c : 4 + c, o : o + 128] = total[0:1]

        first = []
        for d in range(1, rsize):
            to = lax.rem(place + d, rsize)
            first.append(
                send(msg.at[k, to], got1.at[k, place], s1s.at[k, d - 1], s1r.at[k, d - 1], (gx, line0 + to))
            )
        pending.extend(first)
        got1[k, place] = msg[k, place]
        if k < SECTIONS - 1:
            plane_copies = send_planes(k + 1, part.at[k])
            gather_plane(part.at[k], 0)
        for copy in first:
            copy.wait_recv()
        tiles = [got1[k, t] for t in range(rsize)]
        coefs = [coefficients(x) for x in tiles]
        e = jnp.where(sub == 6, 1.0, 0.0)
        starts = []
        for t in range(rsize):
            starts.append(e)
            e = down(tiles[t], coefs[t][0], e)
        l = jnp.where(sub == 7, 1.0, 0.0)
        for t in reversed(range(rsize)):
            l = up(tiles[t], coefs[t][1], coefs[t][2], starts[t], l)
        whole = jnp.where(
            (sub < 3) | (sub == 6),
            e,
            jnp.where((sub == 7) & (col < width // 2), pltpu.roll(l, 1, 0), l),
        )
        own2[k] = whole
        got2[k, line] = whole
        second = []
        for d in range(1, rows_n):
            to = lax.rem(line + d, rows_n)
            second.append(
                send(own2.at[k], got2.at[k, line], s2s.at[k, d - 1], s2r.at[k, d - 1], (gx, to * rsize + place))
            )
        pending.extend(second)
        for copy in second:
            copy.wait_recv()
        maps = [got2[k, q] for q in range(rows_n)]
        mcoefs = [coefficients(x) for x in maps]
        e = jnp.zeros((8, width), F32)
        e_row = jnp.zeros((8, width), F32)
        starts = []
        for q in range(rows_n):
            starts.append(e)
            e_row = jnp.where(line == q, e, e_row)
            e = down(maps[q], mcoefs[q][0], e)
        l = jnp.zeros((8, width), F32)
        l_row = jnp.zeros((8, width), F32)
        for q in reversed(range(rows_n)):
            l_row = jnp.where(line == q, l, l_row)
            l = up(maps[q], mcoefs[q][1], mcoefs[q][2], starts[q], l)
        e = jnp.where(sub < 3, e_row, 0.0)
        starts = []
        for t in range(rsize):
            starts.append(e)
            e = down(tiles[t], coefs[t][0], e)
        l = l_row
        for t in reversed(range(rsize)):
            ans[k, t] = jnp.where(sub < 3, starts[t], jnp.where(sub < 6, l, 0.0))
            l = up(tiles[t], coefs[t][1], coefs[t][2], starts[t], l)
        third = []
        for d in range(rsize):
            to = lax.rem(place + d, rsize)
            mate = line0 + to
            if d > 0:
                third.append(
                    send(ans.at[k, to], el.at[k, 0, place], s3s.at[k, 0, d], s3r.at[k, 0, d], (gx, mate))
                )
            if k < SECTIONS - 1:
                third.append(
                    send(ans.at[k, to], el.at[k, 1, place], s3s.at[k, 1, d], s3r.at[k, 1, d], (east, mate))
                )
                third.append(
                    send(ans.at[k, to], el.at[k, 2, place], s3s.at[k, 2, d], s3r.at[k, 2, d], (west, mate))
                )
        pending.extend(third)
        el[k, 0, place] = ans[k, place]
        if k < SECTIONS - 1:
            for copy in plane_copies:
                copy.wait_recv()
            gather_plane(planes.at[k + 1, 1], 1)
        else:
            for copy in trips:
                copy.wait_recv()
            part_out[:, 0:RESIDENT] = moved[0:3, 0:RESIDENT]
            part_out[:, RESIDENT : RESIDENT + CAP] = mig[0, 0:3, :]
            part_out[:, RESIDENT + CAP : RESIDENT + 2 * CAP] = mig[1, 0:3, :] * above_edge
            part_out[:, RESIDENT + 2 * CAP : RESIDENT + 3 * CAP] = mig[2, 0:3, :] * below_edge
        for copy in third:
            copy.wait_recv()

    rows = plane_rows(SECTIONS - 1, 0)
    k = SECTIONS - 1
    for c in range(comps):
        field_out[c] = part[k, c] + alpha[k] * rows[c : c + 1] + beta[k] * rows[3 + c : 4 + c]
    for copy in pending:
        copy.wait_send()


def on_device(
    velocity, y_metric, forward_rate, backward_rate, pivot_inv,
    particle_vel, particle_cell, particle_offset, inverse_tau, outgoing_count,
):
    comps, _, cy, cz = velocity.shape
    slots = particle_vel.shape[1]
    nx, lanes = lax.axis_size("gx"), lax.axis_size("gy")
    rsize = row_size(lanes)
    rows_n = lanes // rsize
    width = cz // rsize
    vmem, smem = pltpu.VMEM, pl.BlockSpec(memory_space=pltpu.SMEM)
    whole = pl.BlockSpec(memory_space=pltpu.VMEM)
    dma = pltpu.SemaphoreType.DMA
    scratch = [
        vmem((cz, slots), BF16),
        vmem((4 * comps * cy, cz), BF16),
        vmem((64, cz), BF16),
        vmem((2 * comps * cy, slots), BF16),
        vmem((comps * cy, cz), F32),
        vmem((8, slots), F32),
        vmem((cy, slots), F32),
        vmem((cy, slots), F32),
        vmem((SECTIONS, 8, slots), F32),
        vmem((8, slots), F32),
        vmem((8, slots), F32),
        vmem((1, slots), F32),
        vmem((8, slots), F32),
        vmem((SECTIONS, cy, cy, 128), F32),
        vmem((SECTIONS, cy, 128), F32),
        vmem((SECTIONS, cy, cz), F32),
        vmem((SECTIONS, cy, cz), F32),
        vmem((cy, cz), F32),
        vmem((cy, 128), F32),
        vmem((SECTIONS, comps, cy, cz), F32),
        vmem((SECTIONS, 2, comps, cy, cz), F32),
        vmem((comps, cy, cz), F32),
        vmem((comps, cy, cz), F32),
        vmem((8, cz), F32),
        vmem((3, 8, cz), F32),
        vmem((SECTIONS, rsize, 8, width), F32),
        vmem((SECTIONS, rsize, 8, width), F32),
        vmem((SECTIONS, rows_n, 8, width), F32),
        vmem((SECTIONS, 8, width), F32),
        vmem((SECTIONS, rsize, 8, width), F32),
        vmem((SECTIONS, 3, rsize, 8, width), F32),
        vmem((3, 8, CAP), F32),
        dma((SECTIONS, rsize - 1)), dma((SECTIONS, rsize - 1)),
        dma((SECTIONS, rows_n - 1)), dma((SECTIONS, rows_n - 1)),
        dma((SECTIONS, 3, rsize)), dma((SECTIONS, 3, rsize)),
        dma((SECTIONS, 2)), dma((SECTIONS, 2)),
        dma((3,)), dma((3,)), dma((3,)), dma((3,)),
    ]
    field, moved = pl.pallas_call(
        functools.partial(kernel, (nx, lanes, rsize)),
        out_shape=(
            jax.ShapeDtypeStruct((comps, cy, cz), F32),
            jax.ShapeDtypeStruct((comps, slots), F32),
        ),
        in_specs=[whole, smem, smem, smem, smem, whole, whole, whole, whole, smem],
        out_specs=(whole, whole),
        scratch_shapes=scratch,
        compiler_params=pltpu.CompilerParams(
            collective_id=0, has_side_effects=True, vmem_limit_bytes=48 * 1024 * 1024
        ),
        name="channel_sections",
    )(
        velocity.reshape(comps, cy, cz),
        y_metric,
        forward_rate,
        backward_rate,
        pivot_inv,
        particle_vel,
        particle_cell.reshape(1, slots),
        particle_offset,
        inverse_tau.reshape(1, slots),
        outgoing_count.reshape(3),
    )
    return field.reshape(velocity.shape), moved


def solution(mesh):
    return jax.shard_map(
        on_device,
        mesh=mesh,
        in_specs=(
            P(None, "gx", "gy", None),
            P("gy"),
            P(None, "gy"),
            P(None, "gy"),
            P(None, "gy"),
            P(None, ("gx", "gy")),
            P(("gx", "gy")),
            P(None, ("gx", "gy")),
            P(("gx", "gy")),
            P("gx", "gy", None),
        ),
        out_specs=(P(None, "gx", "gy", None), P(None, ("gx", "gy"))),
        check_vma=False,
    )
```

```python
import functools

import jax
import jax.numpy as jnp
from jax import lax
from jax.experimental import pallas as pl
from jax.experimental.pallas import tpu as pltpu
from jax.sharding import PartitionSpec as P

RESIDENT = 2048
CAP = 512
SECTIONS = 3
SECTION_WEIGHTS = (8.0 / 15.0, 5.0 / 12.0, 3.0 / 4.0)
TIME_STEP = 0.3
STREAM_SCALE = 2.0
SPAN_SCALE = 2.0
COUPLING = 0.5
CHUNK = 512
MESH = pl.DeviceIdType.MESH
F32 = jnp.float32
BF16 = jnp.bfloat16


def row_size(lanes):
    return 8 if lanes == 32 else max(2, lanes // 2)


def halves(x):
    high = x.astype(BF16)
    return high, (x - high.astype(F32)).astype(BF16)


def kernel(
    dims,
    vel_in, metric, fwd, bwd, piv, pvel_in, cell_in, offset_in, tau_in, count,
    field_out, part_out,
    vel, pvel, cell, offset, tau, inputs_sem,
    onehot, table, el_table, scat, accum, wts, ymask, ywt, ab, speed, fluid, live_ref, moved,
    solve_cols, carry_col, alpha, beta, ymet, unit_rows,
    part, planes, uref, rhs_ref, edge, edge_in, msg, got1, got2, own2, ans, el, mig,
    s1s, s1r, s2s, s2r, s3s, s3r, pls, plr, eds, edr, mgs, mgr,
):
    nx, lanes, rsize = dims
    rows_n = lanes // rsize
    comps, cy, cz = vel_in.shape
    width = cz // rsize
    slots = pvel_in.shape[1]
    chunk = min(CHUNK, slots)
    steps = slots // chunk
    last = cy - 1
    rows6 = 2 * comps * cy
    gx = lax.axis_index("gx")
    gy = lax.axis_index("gy")
    place = lax.rem(gy, rsize)
    line = gy // rsize
    line0 = line * rsize
    west = lax.rem(gx + nx - 1, nx)
    east = lax.rem(gx + 1, nx)
    south = lax.rem(gy + lanes - 1, lanes)
    north = lax.rem(gy + 1, lanes)

    def send(src, dst, ssem, rsem, to):
        copy = pltpu.make_async_remote_copy(
            src_ref=src, dst_ref=dst, send_sem=ssem, recv_sem=rsem,
            device_id=to, device_id_type=MESH,
        )
        copy.start()
        return copy

    loads = [
        pltpu.make_async_copy(src, dst, inputs_sem.at[n])
        for n, (src, dst) in enumerate(
            ((vel_in, vel), (cell_in, cell), (offset_in, offset), (pvel_in, pvel), (tau_in, tau))
        )
    ]
    for load in loads:
        load.start()
    partners = []
    for d in range(1, rsize):
        partners.append((gx, line0 + lax.rem(place + d, rsize)))
    for d in range(1, rows_n):
        partners.append((gx, lax.rem(line + d, rows_n) * rsize + place))
    partners += [(west, gy), (east, gy), (gx, south), (gx, north), (west, south), (east, north)]
    barrier = pltpu.get_barrier_semaphore()
    for to in partners:
        pl.semaphore_signal(barrier, inc=1, device_id=to, device_id_type=MESH)

    loads[0].wait()
    for c in range(comps):
        edge[c : c + 1, :] = vel[c, last : last + 1, :]
        edge[3 + c : 4 + c, :] = vel[c, 0:1, :]
    edge[6:8, :] = jnp.zeros((2, cz), F32)
    for n, value in enumerate((piv[0, last], bwd[0, last], piv[1, last], bwd[1, last])):
        edge[6:7, n * 128 : (n + 1) * 128] = jnp.full((1, 128), value, F32)

    pl.semaphore_wait(barrier, len(partners))

    pending = []

    def send_planes(k, src):
        a = send(src, planes.at[k, 1], pls.at[k, 0], plr.at[k, 0], (west, gy))
        b = send(src, planes.at[k, 0], pls.at[k, 1], plr.at[k, 1], (east, gy))
        pending.extend([a, b])
        return a, b

    plane_copies = send_planes(0, vel)
    edge_copies = [
        send(edge, edge_in.at[0], eds.at[0], edr.at[0], (gx, north)),
        send(edge, edge_in.at[1], eds.at[1], edr.at[1], (gx, south)),
        send(edge, edge_in.at[2], eds.at[2], edr.at[2], (west, south)),
    ]
    pending.extend(edge_copies)

    for load in loads[1:]:
        load.wait()
    row16 = lax.broadcasted_iota(jnp.int32, (cy, chunk), 0)
    lane = lax.broadcasted_iota(jnp.int32, (1, chunk), 1)
    zblock = min(256, cz)
    zrow = lax.broadcasted_iota(jnp.int32, (zblock, chunk), 0)
    c0, c1, c2 = count[0], count[1], count[2]
    speed[...] = jnp.zeros_like(speed)
    fluid[...] = jnp.zeros_like(fluid)

    def prepare(i, _):
        at = pl.ds(pl.multiple_of(i * chunk, chunk), chunk)
        where = cell[at].reshape(1, chunk)
        zpos = lax.rem(where, cz)
        ypos = lax.rem(lax.div(where, cz), cy)
        for n in range(cz // zblock):
            onehot[n * zblock : (n + 1) * zblock, at] = jnp.where(
                zrow + n * zblock == zpos, 1.0, 0.0
            ).astype(BF16)
        ox, oy, oz = offset[0:1, at], offset[1:2, at], offset[2:3, at]
        here = row16 == ypos
        above = row16 == ypos + 1
        ymask[:, at] = jnp.where(here, 1.0, 0.0)
        ywt[:, at] = jnp.where(here, 1.0 - oy, jnp.where(above, oy, 0.0))
        wts[0:1, at] = (1.0 - ox) * (1.0 - oz)
        wts[1:2, at] = (1.0 - ox) * oz
        wts[2:3, at] = ox * (1.0 - oz)
        wts[3:4, at] = ox * oz
        wts[4:5, at] = jnp.where(ypos == last, oy, 0.0)
        slot = lane + i * chunk
        out = slot - RESIDENT
        turn = jnp.where(out < CAP, out, jnp.where(out < 2 * CAP, out - CAP, out - 2 * CAP))
        limit = jnp.where(out < CAP, c0, jnp.where(out < 2 * CAP, c1, c2))
        live_ref[:, at] = jnp.where((out < 0) | (turn < limit), 1.0, 0.0)
        speed[0:3, at] = pvel[:, at]
        return 0

    lax.fori_loop(0, steps, prepare, 0)

    lane128 = lax.broadcasted_iota(jnp.int32, (1, 128), 1)
    for k in range(SECTIONS):
        g = jnp.zeros((1, 128), F32)
        gs = []
        for j in range(cy):
            g = jnp.where(lane128 == j, 1.0, 0.0) + fwd[k, j] * g
            gs.append(g)
        u = jnp.zeros((1, 128), F32)
        for j in reversed(range(cy)):
            u = piv[k, j] * gs[j] + bwd[k, j] * u
            unit_rows[j : j + 1, :] = u
        block = unit_rows[...]
        for i in range(cy):
            solve_cols[k, i] = jnp.broadcast_to(block[:, i : i + 1], (cy, 128))
        alpha[k] = jnp.broadcast_to(block[:, 0:1] * fwd[k, 0], (cy, cz))
        weight = jnp.float32(1.0)
        shrink = jnp.float32(1.0)
        for j in reversed(range(cy)):
            carry_col[k, j : j + 1, :] = jnp.full((1, 128), weight, F32)
            weight = weight * fwd[k, j]
            shrink = shrink * bwd[k, j]
            beta[k, j : j + 1, :] = jnp.full((1, cz), shrink, F32)
        for t in range(rsize):
            msg[k, t, 6:7, :] = jnp.full((1, width), weight, F32)
            half = lax.broadcasted_iota(jnp.int32, (1, width), 1) < width // 2
            msg[k, t, 7:8, :] = jnp.where(half, alpha[k, 0:1, 0:width], shrink)
    for j in range(cy):
        ymet[j : j + 1, :] = jnp.full((1, cz), 0.5 * metric[j], F32)

    def responses(i, _):
        at = pl.ds(pl.multiple_of(i * chunk, chunk), chunk)
        top = wts[4:5, at]
        w = ywt[:, at]
        zero = jnp.zeros((3, chunk), F32)
        two = jnp.zeros((2, chunk), F32)
        ab[0, :, at] = jnp.concatenate([zero, top, top, top, two], axis=0)
        for k in range(1, SECTIONS):
            a = jnp.sum(w * alpha[k - 1, :, 0:1], axis=0, keepdims=True)
            b = jnp.sum(w * beta[k - 1, :, 0:1], axis=0, keepdims=True) + top
            ab[k, :, at] = jnp.concatenate([a, a, a, b, b, b, two], axis=0)
        return 0

    lax.fori_loop(0, steps, responses, 0)

    def gather_plane(source, side):
        for c in range(comps):
            x = source[c]
            high, low = halves(x)
            table[c * cy : (c + 1) * cy, :] = high
            table[rows6 + c * cy : rows6 + (c + 1) * cy, :] = low
            high, low = halves(pltpu.roll(x, cz - 1, 1))
            at = (comps + c) * cy
            table[at : at + cy, :] = high
            table[rows6 + at : rows6 + at + cy, :] = low

        def one(i):
            at = slice(i * chunk, (i + 1) * chunk)
            hot = onehot[:, at]
            got = jnp.dot(table[...], hot, preferred_element_type=F32)
            got = got[0:rows6] + got[rows6 : 2 * rows6]
            w0 = wts[2 * side : 2 * side + 1, at]
            w1 = wts[2 * side + 1 : 2 * side + 2, at]
            w = ywt[:, at]
            rows = []
            for c in range(comps):
                near = got[c * cy : (c + 1) * cy]
                far = got[(comps + c) * cy : (comps + c + 1) * cy]
                rows.append(jnp.sum((w0 * near + w1 * far) * w, axis=0, keepdims=True))
            value = jnp.concatenate(rows, axis=0)
            if side == 0:
                fluid[0:3, at] = value
            else:
                fluid[0:3, at] = fluid[0:3, at] + value

        for i in range(steps):
            one(i)

    sub = lax.broadcasted_iota(jnp.int32, (8, width), 0)
    col = lax.broadcasted_iota(jnp.int32, (8, width), 1)

    def coefficients(x):
        grow = jnp.broadcast_to(x[6:7], (8, width))
        seven = jnp.broadcast_to(x[7:8], (8, width))
        other = pltpu.roll(seven, width // 2, 1)
        mixed = jnp.where(col < width // 2, seven, other)
        shrink = jnp.where(col < width // 2, other, seven)
        return grow, mixed, shrink

    def lifted(e):
        return jnp.where((sub >= 3) & (sub < 6), pltpu.roll(e, 3, 0), jnp.where(sub == 6, e, 0.0))

    def down(x, grow, e):
        return jnp.where(sub < 3, x, 0.0) + grow * e

    def up(x, mixed, shrink, e, l):
        return jnp.where((sub >= 3) & (sub < 6), x, 0.0) + mixed * lifted(e) + shrink * l

    def plane_rows(k, slot):
        return jnp.concatenate([el[k, slot, t] for t in range(rsize)], axis=1)

    below_edge = jnp.where(gy > 0, 1.0, 0.0).astype(F32)
    above_edge = jnp.where(gy < lanes - 1, 1.0, 0.0).astype(F32)

    gather_plane(vel, 0)
    for copy in edge_copies:
        copy.wait_recv()
    plane_copies[0].wait_recv()
    gather_plane(planes.at[0, 1], 1)
    behind = []

    for k in range(SECTIONS):
        step = TIME_STEP * SECTION_WEIGHTS[k]
        if k == 0:
            sub_full = lax.broadcasted_iota(jnp.int32, (8, cz), 0)
            upper = jnp.where((sub_full >= 3) & (sub_full < 6), 1.0, 0.0) * above_edge
            lower = jnp.where(sub_full < 3, 1.0, 0.0) * below_edge
            own = edge_in[0] * lower + edge_in[1] * upper
            plus = edge_in[2] * upper
        else:
            own, plus = plane_rows(k - 1, 0), plane_rows(k - 1, 2)
        pair = jnp.concatenate([own, plus], axis=0)
        high, low = halves(pair)
        el_table[0:16, :] = high
        el_table[32:48, :] = low
        high, low = halves(pltpu.roll(pair, cz - 1, 1))
        el_table[16:32, :] = high
        el_table[48:64, :] = low

        def push(i, k=k, step=step):
            at = slice(i * chunk, (i + 1) * chunk)
            hot = onehot[:, at]
            got = jnp.dot(el_table[...], hot, preferred_element_type=F32)
            got = got[0:32] + got[32:64]
            mix = (
                wts[0:1, at] * got[0:8]
                + wts[2:3, at] * got[8:16]
                + wts[1:2, at] * got[16:24]
                + wts[3:4, at] * got[24:32]
            ) * ab[k, :, at]
            flow = fluid[:, at] + mix + pltpu.roll(mix, 5, 0)
            now = speed[:, at]
            drag = tau[at].reshape(1, chunk) * (flow - now)
            speed[:, at] = now + step * drag
            share = drag * (-COUPLING * live_ref[:, at])
            mask = ymask[:, at]
            for c in range(comps):
                one = share[c : c + 1]
                head = one.astype(BF16).astype(F32)
                scat[c * cy : (c + 1) * cy, at] = (mask * head).astype(BF16)
                scat[(comps + c) * cy : (comps + c + 1) * cy, at] = (mask * (one - head)).astype(BF16)

        for i in range(steps):
            push(i)

        if k == SECTIONS - 1:
            moved[...] = speed[...] * live_ref[...]
            trips = [
                send(moved.at[:, RESIDENT : RESIDENT + CAP], mig.at[0], mgs.at[0], mgr.at[0], (east, gy)),
                send(moved.at[:, RESIDENT + CAP : RESIDENT + 2 * CAP], mig.at[1], mgs.at[1], mgr.at[1], (gx, south)),
                send(moved.at[:, RESIDENT + 2 * CAP : RESIDENT + 3 * CAP], mig.at[2], mgs.at[2], mgr.at[2], (gx, north)),
            ]
            pending.extend(trips)

        def gathered(n):
            at = slice(n * zblock, (n + 1) * zblock)
            both = lax.dot_general(
                scat[...], onehot[at, :], (((1,), (1,)), ((), ())), preferred_element_type=F32
            )
            half = comps * cy
            accum[:, at] = both[0:half] + both[half : 2 * half]

        for n in range(cz // zblock):
            gathered(n)

        plane_copies[1].wait_recv()
        for copy in behind:
            copy.wait_recv()
        minus = plane_rows(k - 1, 1) if k > 0 else None

        def plane(source, c, rows):
            if k == 0:
                return source[c]
            return source[c] + alpha[k - 1] * rows[c : c + 1] + beta[k - 1] * rows[3 + c : 4 + c]

        for c in range(comps):
            uref[c] = plane(vel if k == 0 else part.at[k - 1], c, own)
        rowz = lax.broadcasted_iota(jnp.int32, (cy, cz), 0)
        for c in range(comps):
            u = uref[c]
            slope_x = (plane(planes.at[k, 1], c, plus) - plane(planes.at[k, 0], c, minus)) * (
                0.5 * STREAM_SCALE
            )
            slope_z = (pltpu.roll(u, cz - 1, 1) - pltpu.roll(u, 1, 1)) * (0.5 * SPAN_SCALE)
            if k == 0:
                under = own[c : c + 1]
            else:
                rate = edge_in[0, 6:7, :]
                base = 256 * (k - 1)
                pv = jnp.concatenate([rate[:, base : base + 128]] * (cz // 128), axis=1)
                bv = jnp.concatenate([rate[:, base + 128 : base + 256]] * (cz // 128), axis=1)
                under = (pv * own[c : c + 1] + bv * u[0:1]) * below_edge
            upper_y = jnp.where(rowz == last, own[3 + c : 4 + c], pltpu.roll(u, cy - 1, 0))
            lower_y = jnp.where(rowz == 0, under, pltpu.roll(u, 1, 0))
            slope_y = (upper_y - lower_y) * ymet[...]
            convection = -(uref[0] * slope_x + uref[1] * slope_y + uref[2] * slope_z)
            rhs_ref[c] = u + step * (convection + accum[c * cy : (c + 1) * cy, :])

        for c in range(comps):
            for z in range(cz // 128):
                at = slice(z * 128, (z + 1) * 128)
                total = None
                for i in range(cy):
                    term = solve_cols[k, i] * rhs_ref[c, i : i + 1, at]
                    total = term if total is None else total + term
                part[k, c, :, at] = total
                leave = jnp.sum(carry_col[k] * rhs_ref[c, :, at], axis=0, keepdims=True)
                t, o = (z * 128) // width, (z * 128) % width
                msg[k, t, c : c + 1, o : o + 128] = leave
                msg[k, t, 3 + c : 4 + c, o : o + 128] = total[0:1]

        first = []
        for d in range(1, rsize):
            to = lax.rem(place + d, rsize)
            first.append(
                send(msg.at[k, to], got1.at[k, place], s1s.at[k, d - 1], s1r.at[k, d - 1], (gx, line0 + to))
            )
        pending.extend(first)
        got1[k, place] = msg[k, place]
        if k < SECTIONS - 1:
            plane_copies = send_planes(k + 1, part.at[k])
            gather_plane(part.at[k], 0)
        for copy in first:
            copy.wait_recv()
        tiles = [got1[k, t] for t in range(rsize)]
        coefs = [coefficients(x) for x in tiles]
        e = jnp.where(sub == 6, 1.0, 0.0)
        starts = []
        for t in range(rsize):
            starts.append(e)
            e = down(tiles[t], coefs[t][0], e)
        l = jnp.where(sub == 7, 1.0, 0.0)
        for t in reversed(range(rsize)):
            l = up(tiles[t], coefs[t][1], coefs[t][2], starts[t], l)
        whole = jnp.where(
            (sub < 3) | (sub == 6),
            e,
            jnp.where((sub == 7) & (col < width // 2), pltpu.roll(l, 1, 0), l),
        )
        own2[k] = whole
        got2[k, line] = whole
        second = []
        for d in range(1, rows_n):
            to = lax.rem(line + d, rows_n)
            second.append(
                send(own2.at[k], got2.at[k, line], s2s.at[k, d - 1], s2r.at[k, d - 1], (gx, to * rsize + place))
            )
        pending.extend(second)
        for copy in second:
            copy.wait_recv()
        maps = [got2[k, q] for q in range(rows_n)]
        mcoefs = [coefficients(x) for x in maps]
        e = jnp.zeros((8, width), F32)
        e_row = jnp.zeros((8, width), F32)
        starts = []
        for q in range(rows_n):
            starts.append(e)
            e_row = jnp.where(line == q, e, e_row)
            e = down(maps[q], mcoefs[q][0], e)
        l = jnp.zeros((8, width), F32)
        l_row = jnp.zeros((8, width), F32)
        for q in reversed(range(rows_n)):
            l_row = jnp.where(line == q, l, l_row)
            l = up(maps[q], mcoefs[q][1], mcoefs[q][2], starts[q], l)
        e = jnp.where(sub < 3, e_row, 0.0)
        starts = []
        for t in range(rsize):
            starts.append(e)
            e = down(tiles[t], coefs[t][0], e)
        l = l_row
        for t in reversed(range(rsize)):
            ans[k, t] = jnp.where(sub < 3, starts[t], jnp.where(sub < 6, l, 0.0))
            l = up(tiles[t], coefs[t][1], coefs[t][2], starts[t], l)
        third = {slot: [] for slot in range(3)}
        routes = [(0, gx), (2, west), (1, east)] if k < SECTIONS - 1 else [(0, gx)]
        for slot, column in routes:
            for d in range(1 if slot == 0 else 0, rsize):
                to = lax.rem(place + d, rsize)
                third[slot].append(
                    send(ans.at[k, to], el.at[k, slot, place], s3s.at[k, slot, d], s3r.at[k, slot, d], (column, line0 + to))
                )
        pending.extend(third[0] + third[1] + third[2])
        el[k, 0, place] = ans[k, place]
        if k < SECTIONS - 1:
            plane_copies[0].wait_recv()
            gather_plane(planes.at[k + 1, 1], 1)
        else:
            for copy in trips:
                copy.wait_recv()
            part_out[:, 0:RESIDENT] = moved[0:3, 0:RESIDENT]
            part_out[:, RESIDENT : RESIDENT + CAP] = mig[0, 0:3, :]
            part_out[:, RESIDENT + CAP : RESIDENT + 2 * CAP] = mig[1, 0:3, :] * above_edge
            part_out[:, RESIDENT + 2 * CAP : RESIDENT + 3 * CAP] = mig[2, 0:3, :] * below_edge
        for copy in third[0] + third[2]:
            copy.wait_recv()
        behind = third[1]

    rows = plane_rows(SECTIONS - 1, 0)
    k = SECTIONS - 1
    for c in range(comps):
        field_out[c] = part[k, c] + alpha[k] * rows[c : c + 1] + beta[k] * rows[3 + c : 4 + c]
    for copy in pending:
        copy.wait_send()


def on_device(
    velocity, y_metric, forward_rate, backward_rate, pivot_inv,
    particle_vel, particle_cell, particle_offset, inverse_tau, outgoing_count,
):
    comps, _, cy, cz = velocity.shape
    slots = particle_vel.shape[1]
    nx, lanes = lax.axis_size("gx"), lax.axis_size("gy")
    rsize = row_size(lanes)
    rows_n = lanes // rsize
    width = cz // rsize
    vmem, smem = pltpu.VMEM, pl.BlockSpec(memory_space=pltpu.SMEM)
    whole = pl.BlockSpec(memory_space=pltpu.VMEM)
    dma = pltpu.SemaphoreType.DMA
    far = pl.BlockSpec(memory_space=pltpu.HBM)

    def stay(x):
        return pltpu.with_memory_space_constraint(x, pltpu.HBM)

    scratch = [
        vmem((comps, cy, cz), F32), vmem((comps, slots), F32), vmem((slots,), jnp.int32),
        vmem((3, slots), F32), vmem((slots,), F32), dma((5,)),
        vmem((cz, slots), BF16),
        vmem((4 * comps * cy, cz), BF16),
        vmem((64, cz), BF16),
        vmem((2 * comps * cy, slots), BF16),
        vmem((comps * cy, cz), F32),
        vmem((8, slots), F32),
        vmem((cy, slots), F32),
        vmem((cy, slots), F32),
        vmem((SECTIONS, 8, slots), F32),
        vmem((8, slots), F32),
        vmem((8, slots), F32),
        vmem((1, slots), F32),
        vmem((8, slots), F32),
        vmem((SECTIONS, cy, cy, 128), F32),
        vmem((SECTIONS, cy, 128), F32),
        vmem((SECTIONS, cy, cz), F32),
        vmem((SECTIONS, cy, cz), F32),
        vmem((cy, cz), F32),
        vmem((cy, 128), F32),
        vmem((SECTIONS, comps, cy, cz), F32),
        vmem((SECTIONS, 2, comps, cy, cz), F32),
        vmem((comps, cy, cz), F32),
        vmem((comps, cy, cz), F32),
        vmem((8, cz), F32),
        vmem((3, 8, cz), F32),
        vmem((SECTIONS, rsize, 8, width), F32),
        vmem((SECTIONS, rsize, 8, width), F32),
        vmem((SECTIONS, rows_n, 8, width), F32),
        vmem((SECTIONS, 8, width), F32),
        vmem((SECTIONS, rsize, 8, width), F32),
        vmem((SECTIONS, 3, rsize, 8, width), F32),
        vmem((3, 8, CAP), F32),
        dma((SECTIONS, rsize - 1)), dma((SECTIONS, rsize - 1)),
        dma((SECTIONS, rows_n - 1)), dma((SECTIONS, rows_n - 1)),
        dma((SECTIONS, 3, rsize)), dma((SECTIONS, 3, rsize)),
        dma((SECTIONS, 2)), dma((SECTIONS, 2)),
        dma((3,)), dma((3,)), dma((3,)), dma((3,)),
    ]
    field, moved = pl.pallas_call(
        functools.partial(kernel, (nx, lanes, rsize)),
        out_shape=(
            jax.ShapeDtypeStruct((comps, cy, cz), F32),
            jax.ShapeDtypeStruct((comps, slots), F32),
        ),
        in_specs=[far, smem, smem, smem, smem, far, far, far, far, smem],
        out_specs=(whole, whole),
        scratch_shapes=scratch,
        compiler_params=pltpu.CompilerParams(
            collective_id=0, has_side_effects=True, vmem_limit_bytes=48 * 1024 * 1024
        ),
        name="channel_sections",
    )(
        stay(velocity.reshape(comps, cy, cz)),
        stay(y_metric),
        stay(forward_rate),
        stay(backward_rate),
        stay(pivot_inv),
        stay(particle_vel),
        stay(particle_cell),
        stay(particle_offset),
        stay(inverse_tau),
        stay(outgoing_count.reshape(3)),
    )
    return field.reshape(velocity.shape), moved


def solution(mesh):
    return jax.shard_map(
        on_device,
        mesh=mesh,
        in_specs=(
            P(None, "gx", "gy", None),
            P("gy"),
            P(None, "gy"),
            P(None, "gy"),
            P(None, "gy"),
            P(None, ("gx", "gy")),
            P(("gx", "gy")),
            P(None, ("gx", "gy")),
            P(("gx", "gy")),
            P("gx", "gy", None),
        ),
        out_specs=(P(None, "gx", "gy", None), P(None, ("gx", "gy"))),
        check_vma=False,
    )
```

```python
import functools

import jax
import jax.numpy as jnp
from jax import lax
from jax.experimental import pallas as pl
from jax.experimental.pallas import tpu as pltpu
from jax.sharding import PartitionSpec as P

RESIDENT = 2048
CAP = 512
SECTIONS = 3
SECTION_WEIGHTS = (8.0 / 15.0, 5.0 / 12.0, 3.0 / 4.0)
TIME_STEP = 0.3
STREAM_SCALE = 2.0
SPAN_SCALE = 2.0
COUPLING = 0.5
CHUNK = 512
MESH = pl.DeviceIdType.MESH
F32 = jnp.float32
BF16 = jnp.bfloat16


def row_size(lanes):
    return 8 if lanes == 32 else max(2, lanes // 2)


def halves(x):
    high = x.astype(BF16)
    return high, (x - high.astype(F32)).astype(BF16)


def kernel(
    dims,
    vel_in, metric_in, fwd_in, bwd_in, piv_in, pvel_in, cell_in, offset_in, tau_in, count_in,
    field_out, part_out,
    vel, pvel, cell, offset, tau, inputs_sem,
    sm_metric, sm_fwd, sm_bwd, sm_piv, sm_count, onehot, hot_rows, table, scat, accum, wts, ymask, ywt, ab, speed, fluid, live_ref, moved,
    solve_cols, carry_col, alpha, beta, ymet, unit_rows,
    part, planes, uref, rhs_ref, edge, edge_in, msg, got1, got2, own2, ans, el, mig,
    s1s, s1r, s2s, s2r, s3s, s3r, pls, plr, eds, edr, mgs, mgr,
):
    nx, lanes, rsize = dims
    metric, fwd, bwd, piv, count = sm_metric, sm_fwd, sm_bwd, sm_piv, sm_count
    rows_n = lanes // rsize
    comps, cy, cz = vel_in.shape
    width = cz // rsize
    slots = pvel_in.shape[1]
    chunk = min(CHUNK, slots)
    steps = slots // chunk
    last = cy - 1
    rows6 = 2 * comps * cy
    gx = lax.axis_index("gx")
    gy = lax.axis_index("gy")
    place = lax.rem(gy, rsize)
    line = gy // rsize
    line0 = line * rsize
    west = lax.rem(gx + nx - 1, nx)
    east = lax.rem(gx + 1, nx)
    south = lax.rem(gy + lanes - 1, lanes)
    north = lax.rem(gy + 1, lanes)

    def send(src, dst, ssem, rsem, to):
        copy = pltpu.make_async_remote_copy(
            src_ref=src, dst_ref=dst, send_sem=ssem, recv_sem=rsem,
            device_id=to, device_id_type=MESH,
        )
        copy.start()
        return copy

    loads = [
        pltpu.make_async_copy(src, dst, inputs_sem.at[n])
        for n, (src, dst) in enumerate(
            (
                (vel_in, vel), (piv_in, piv), (bwd_in, bwd),
                (cell_in, cell), (offset_in, offset), (pvel_in, pvel), (tau_in, tau),
                (fwd_in, fwd), (metric_in, metric), (count_in, count),
            )
        )
    ]
    partners = []
    for d in range(1, rsize):
        partners.append((gx, line0 + lax.rem(place + d, rsize)))
    for d in range(1, rows_n):
        partners.append((gx, lax.rem(line + d, rows_n) * rsize + place))
    partners += [(west, gy), (east, gy), (gx, south), (gx, north), (west, south), (east, north)]
    barrier = pltpu.get_barrier_semaphore()
    for to in partners:
        pl.semaphore_signal(barrier, inc=1, device_id=to, device_id_type=MESH)

    for load in loads:
        load.start()
    for load in loads[:3]:
        load.wait()
    for c in range(comps):
        edge[c : c + 1, :] = vel[c, last : last + 1, :]
        edge[3 + c : 4 + c, :] = vel[c, 0:1, :]
    edge[6:8, :] = jnp.zeros((2, cz), F32)
    for n, value in enumerate((piv[0, last], bwd[0, last], piv[1, last], bwd[1, last])):
        edge[6:7, n * 128 : (n + 1) * 128] = jnp.full((1, 128), value, F32)

    pl.semaphore_wait(barrier, len(partners))

    pending = []

    def send_planes(k, src):
        a = send(src, planes.at[k, 1], pls.at[k, 0], plr.at[k, 0], (west, gy))
        b = send(src, planes.at[k, 0], pls.at[k, 1], plr.at[k, 1], (east, gy))
        pending.extend([a, b])
        return a, b

    plane_copies = send_planes(0, vel)
    edge_copies = [
        send(edge, edge_in.at[0], eds.at[0], edr.at[0], (gx, north)),
        send(edge, edge_in.at[1], eds.at[1], edr.at[1], (gx, south)),
        send(edge, edge_in.at[2], eds.at[2], edr.at[2], (west, south)),
    ]
    pending.extend(edge_copies)

    for load in loads[3:]:
        load.wait()
    row16 = lax.broadcasted_iota(jnp.int32, (cy, chunk), 0)
    lane = lax.broadcasted_iota(jnp.int32, (1, chunk), 1)
    zblock = min(256, cz)
    zrow = lax.broadcasted_iota(jnp.int32, (zblock, chunk), 0)
    c0, c1, c2 = count[0], count[1], count[2]
    speed[...] = jnp.zeros_like(speed)
    fluid[...] = jnp.zeros_like(fluid)

    def prepare(i, _):
        at = pl.ds(pl.multiple_of(i * chunk, chunk), chunk)
        where = cell[at].reshape(1, chunk)
        zpos = lax.rem(where, cz)
        ypos = lax.rem(lax.div(where, cz), cy)
        for n in range(cz // zblock):
            onehot[n * zblock : (n + 1) * zblock, at] = jnp.where(
                zrow + n * zblock == zpos, 1.0, 0.0
            ).astype(BF16)
        ox, oy, oz = offset[0:1, at], offset[1:2, at], offset[2:3, at]
        here = row16 == ypos
        above = row16 == ypos + 1
        ymask[:, at] = jnp.where(here, 1.0, 0.0)
        ywt[:, at] = jnp.where(here, 1.0 - oy, jnp.where(above, oy, 0.0))
        wts[0:1, at] = (1.0 - ox) * (1.0 - oz)
        wts[1:2, at] = (1.0 - ox) * oz
        wts[2:3, at] = ox * (1.0 - oz)
        wts[3:4, at] = ox * oz
        wts[4:5, at] = jnp.where(ypos == last, oy, 0.0)
        slot = lane + i * chunk
        out = slot - RESIDENT
        turn = jnp.where(out < CAP, out, jnp.where(out < 2 * CAP, out - CAP, out - 2 * CAP))
        limit = jnp.where(out < CAP, c0, jnp.where(out < 2 * CAP, c1, c2))
        live_ref[:, at] = jnp.where((out < 0) | (turn < limit), 1.0, 0.0)
        speed[0:3, at] = pvel[:, at]
        return 0

    lax.fori_loop(0, steps, prepare, 0)

    lane128 = lax.broadcasted_iota(jnp.int32, (1, 128), 1)
    for k in range(SECTIONS):
        g = jnp.zeros((1, 128), F32)
        gs = []
        for j in range(cy):
            g = jnp.where(lane128 == j, 1.0, 0.0) + fwd[k, j] * g
            gs.append(g)
        u = jnp.zeros((1, 128), F32)
        for j in reversed(range(cy)):
            u = piv[k, j] * gs[j] + bwd[k, j] * u
            unit_rows[j : j + 1, :] = u
        block = unit_rows[...]
        for i in range(cy):
            solve_cols[k, i] = jnp.broadcast_to(block[:, i : i + 1], (cy, 128))
        alpha[k] = jnp.broadcast_to(block[:, 0:1] * fwd[k, 0], (cy, cz))
        weight = jnp.float32(1.0)
        shrink = jnp.float32(1.0)
        for j in reversed(range(cy)):
            carry_col[k, j : j + 1, :] = jnp.full((1, 128), weight, F32)
            weight = weight * fwd[k, j]
            shrink = shrink * bwd[k, j]
            beta[k, j : j + 1, :] = jnp.full((1, cz), shrink, F32)
        for t in range(rsize):
            msg[k, t, 6:7, :] = jnp.full((1, width), weight, F32)
            half = lax.broadcasted_iota(jnp.int32, (1, width), 1) < width // 2
            msg[k, t, 7:8, :] = jnp.where(half, alpha[k, 0:1, 0:width], shrink)
    for j in range(cy):
        ymet[j : j + 1, :] = jnp.full((1, cz), 0.5 * metric[j], F32)

    def responses(i, _):
        at = pl.ds(pl.multiple_of(i * chunk, chunk), chunk)
        top = wts[4:5, at]
        w = ywt[:, at]
        zero = jnp.zeros((3, chunk), F32)
        two = jnp.zeros((2, chunk), F32)
        ab[0, :, at] = jnp.concatenate([zero, top, top, top, two], axis=0)
        for k in range(1, SECTIONS):
            a = jnp.sum(w * alpha[k - 1, :, 0:1], axis=0, keepdims=True)
            b = jnp.sum(w * beta[k - 1, :, 0:1], axis=0, keepdims=True) + top
            ab[k, :, at] = jnp.concatenate([a, a, a, b, b, b, two], axis=0)
        return 0

    lax.fori_loop(0, steps, responses, 0)

    def fill_table(source):
        for c in range(comps):
            x = source[c]
            high, low = halves(x)
            table[c * cy : (c + 1) * cy, :] = high
            table[rows6 + c * cy : rows6 + (c + 1) * cy, :] = low
            high, low = halves(pltpu.roll(x, cz - 1, 1))
            at = (comps + c) * cy
            table[at : at + cy, :] = high
            table[rows6 + at : rows6 + at + cy, :] = low

    def interpolate(got, side, at):
        got = got[0:rows6] + got[rows6 : 2 * rows6]
        w0 = wts[2 * side : 2 * side + 1, at]
        w1 = wts[2 * side + 1 : 2 * side + 2, at]
        w = ywt[:, at]
        rows = []
        for c in range(comps):
            near = got[c * cy : (c + 1) * cy]
            far = got[(comps + c) * cy : (comps + c + 1) * cy]
            rows.append(jnp.sum((w0 * near + w1 * far) * w, axis=0, keepdims=True))
        value = jnp.concatenate(rows, axis=0)
        if side == 0:
            fluid[0:3, at] = value
        else:
            fluid[0:3, at] = fluid[0:3, at] + value

    def gather_plane(source, side):
        fill_table(source)
        for i in range(steps):
            at = slice(i * chunk, (i + 1) * chunk)
            got = jnp.dot(table[0 : 2 * rows6, :], onehot[:, at], preferred_element_type=F32)
            interpolate(got, side, at)

    sub = lax.broadcasted_iota(jnp.int32, (8, width), 0)
    col = lax.broadcasted_iota(jnp.int32, (8, width), 1)

    def coefficients(x):
        grow = jnp.broadcast_to(x[6:7], (8, width))
        seven = jnp.broadcast_to(x[7:8], (8, width))
        other = pltpu.roll(seven, width // 2, 1)
        mixed = jnp.where(col < width // 2, seven, other)
        shrink = jnp.where(col < width // 2, other, seven)
        return grow, mixed, shrink

    def lifted(e):
        return jnp.where((sub >= 3) & (sub < 6), pltpu.roll(e, 3, 0), jnp.where(sub == 6, e, 0.0))

    def down(x, grow, e):
        return jnp.where(sub < 3, x, 0.0) + grow * e

    def up(x, mixed, shrink, e, l):
        return jnp.where((sub >= 3) & (sub < 6), x, 0.0) + mixed * lifted(e) + shrink * l

    def plane_rows(k, slot):
        return jnp.concatenate([el[k, slot, t] for t in range(rsize)], axis=1)

    below_edge = jnp.where(gy > 0, 1.0, 0.0).astype(F32)
    above_edge = jnp.where(gy < lanes - 1, 1.0, 0.0).astype(F32)

    gather_plane(vel, 0)
    wide = lax.broadcasted_iota(jnp.int32, (128, cz), 1)
    for n in range(slots // 128):
        zpos = lax.rem(cell[n * 128 : (n + 1) * 128].reshape(1, 128), cz)
        column = jnp.transpose(jnp.broadcast_to(zpos.astype(F32), (128, 128))).astype(jnp.int32)
        spread = jnp.concatenate([column] * (cz // 128), axis=1)
        hot_rows[n * 128 : (n + 1) * 128, :] = jnp.where(wide == spread, 1.0, 0.0).astype(BF16)
    for copy in edge_copies:
        copy.wait_recv()
    plane_copies[0].wait_recv()
    fill_table(planes.at[0, 1])
    behind = []

    for k in range(SECTIONS):
        step = TIME_STEP * SECTION_WEIGHTS[k]
        if k == 0:
            sub_full = lax.broadcasted_iota(jnp.int32, (8, cz), 0)
            upper = jnp.where((sub_full >= 3) & (sub_full < 6), 1.0, 0.0) * above_edge
            lower = jnp.where(sub_full < 3, 1.0, 0.0) * below_edge
            own = edge_in[0] * lower + edge_in[1] * upper
            plus = edge_in[2] * upper
        else:
            own, plus = plane_rows(k - 1, 0), plane_rows(k - 1, 2)
        pair = jnp.concatenate([own, plus], axis=0)
        high, low = halves(pair)
        table[2 * rows6 + 0 : 2 * rows6 + 16, :] = high
        table[2 * rows6 + 32 : 2 * rows6 + 48, :] = low
        high, low = halves(pltpu.roll(pair, cz - 1, 1))
        table[2 * rows6 + 16 : 2 * rows6 + 32, :] = high
        table[2 * rows6 + 48 : 2 * rows6 + 64, :] = low

        def push(i, k=k, step=step):
            at = slice(i * chunk, (i + 1) * chunk)
            hot = onehot[:, at]
            base = 2 * rows6 if k else 0
            got = jnp.dot(table[base:, :], hot, preferred_element_type=F32)
            if k == 0:
                interpolate(got, 1, at)
                got = got[2 * rows6 :]
            got = got[0:32] + got[32:64]
            mix = (
                wts[0:1, at] * got[0:8]
                + wts[2:3, at] * got[8:16]
                + wts[1:2, at] * got[16:24]
                + wts[3:4, at] * got[24:32]
            ) * ab[k, :, at]
            flow = fluid[:, at] + mix + pltpu.roll(mix, 5, 0)
            now = speed[:, at]
            drag = tau[at].reshape(1, chunk) * (flow - now)
            speed[:, at] = now + step * drag
            share = drag * (-COUPLING * live_ref[:, at])
            mask = ymask[:, at]
            for c in range(comps):
                one = share[c : c + 1]
                head = one.astype(BF16).astype(F32)
                scat[c * cy : (c + 1) * cy, at] = (mask * head).astype(BF16)
                scat[(comps + c) * cy : (comps + c + 1) * cy, at] = (mask * (one - head)).astype(BF16)

        for i in range(steps):
            push(i)

        if k == SECTIONS - 1:
            moved[...] = speed[...] * live_ref[...]
            trips = [
                send(moved.at[:, RESIDENT : RESIDENT + CAP], mig.at[0], mgs.at[0], mgr.at[0], (east, gy)),
                send(moved.at[:, RESIDENT + CAP : RESIDENT + 2 * CAP], mig.at[1], mgs.at[1], mgr.at[1], (gx, south)),
                send(moved.at[:, RESIDENT + 2 * CAP : RESIDENT + 3 * CAP], mig.at[2], mgs.at[2], mgr.at[2], (gx, north)),
            ]
            pending.extend(trips)

        def gathered(n):
            at = slice(n * zblock, (n + 1) * zblock)
            both = lax.dot_general(
                scat[...], hot_rows[:, at], (((1,), (0,)), ((), ())), preferred_element_type=F32
            )
            half = comps * cy
            accum[:, at] = both[0:half] + both[half : 2 * half]

        for n in range(cz // zblock):
            gathered(n)

        plane_copies[1].wait_recv()
        for copy in behind:
            copy.wait_recv()
        minus = plane_rows(k - 1, 1) if k > 0 else None

        def plane(source, c, rows):
            if k == 0:
                return source[c]
            return source[c] + alpha[k - 1] * rows[c : c + 1] + beta[k - 1] * rows[3 + c : 4 + c]

        for c in range(comps):
            uref[c] = plane(vel if k == 0 else part.at[k - 1], c, own)
        rowz = lax.broadcasted_iota(jnp.int32, (cy, cz), 0)
        for c in range(comps):
            u = uref[c]
            slope_x = (plane(planes.at[k, 1], c, plus) - plane(planes.at[k, 0], c, minus)) * (
                0.5 * STREAM_SCALE
            )
            slope_z = (pltpu.roll(u, cz - 1, 1) - pltpu.roll(u, 1, 1)) * (0.5 * SPAN_SCALE)
            if k == 0:
                under = own[c : c + 1]
            else:
                rate = edge_in[0, 6:7, :]
                base = 256 * (k - 1)
                pv = jnp.concatenate([rate[:, base : base + 128]] * (cz // 128), axis=1)
                bv = jnp.concatenate([rate[:, base + 128 : base + 256]] * (cz // 128), axis=1)
                under = (pv * own[c : c + 1] + bv * u[0:1]) * below_edge
            upper_y = jnp.where(rowz == last, own[3 + c : 4 + c], pltpu.roll(u, cy - 1, 0))
            lower_y = jnp.where(rowz == 0, under, pltpu.roll(u, 1, 0))
            slope_y = (upper_y - lower_y) * ymet[...]
            convection = -(uref[0] * slope_x + uref[1] * slope_y + uref[2] * slope_z)
            rhs_ref[c] = u + step * (convection + accum[c * cy : (c + 1) * cy, :])

        for c in range(comps):
            for z in range(cz // 128):
                at = slice(z * 128, (z + 1) * 128)
                total = None
                for i in range(cy):
                    term = solve_cols[k, i] * rhs_ref[c, i : i + 1, at]
                    total = term if total is None else total + term
                part[k, c, :, at] = total
                leave = jnp.sum(carry_col[k] * rhs_ref[c, :, at], axis=0, keepdims=True)
                t, o = (z * 128) // width, (z * 128) % width
                msg[k, t, c : c + 1, o : o + 128] = leave
                msg[k, t, 3 + c : 4 + c, o : o + 128] = total[0:1]

        first = []
        for d in range(1, rsize):
            to = lax.rem(place + d, rsize)
            first.append(
                send(msg.at[k, to], got1.at[k, place], s1s.at[k, d - 1], s1r.at[k, d - 1], (gx, line0 + to))
            )
        pending.extend(first)
        got1[k, place] = msg[k, place]
        if k < SECTIONS - 1:
            plane_copies = send_planes(k + 1, part.at[k])
            gather_plane(part.at[k], 0)
        for copy in first:
            copy.wait_recv()
        tiles = [got1[k, t] for t in range(rsize)]
        coefs = [coefficients(x) for x in tiles]
        e = jnp.where(sub == 6, 1.0, 0.0)
        starts = []
        for t in range(rsize):
            starts.append(e)
            e = down(tiles[t], coefs[t][0], e)
        l = jnp.where(sub == 7, 1.0, 0.0)
        ends = [None] * rsize
        for t in reversed(range(rsize)):
            ends[t] = l
            l = up(tiles[t], coefs[t][1], coefs[t][2], starts[t], l)
        whole = jnp.where(
            (sub < 3) | (sub == 6),
            e,
            jnp.where((sub == 7) & (col < width // 2), pltpu.roll(l, 1, 0), l),
        )
        own2[k] = whole
        got2[k, line] = whole
        second = []
        for d in range(1, rows_n):
            to = lax.rem(line + d, rows_n)
            second.append(
                send(own2.at[k], got2.at[k, line], s2s.at[k, d - 1], s2r.at[k, d - 1], (gx, to * rsize + place))
            )
        pending.extend(second)
        middle = (sub >= 3) & (sub < 6)
        forms = []
        for t in range(rsize):
            base = jnp.where(sub < 3, starts[t], jnp.where(middle, ends[t], 0.0))
            of_e = jnp.where(sub < 3, starts[t][6:7], jnp.where(middle, ends[t][6:7], 0.0))
            of_l = jnp.where(middle, ends[t][7:8], 0.0)
            forms.append((base, of_e, of_l))
        for copy in second:
            copy.wait_recv()
        maps = [got2[k, q] for q in range(rows_n)]
        mcoefs = [coefficients(x) for x in maps]
        e = jnp.zeros((8, width), F32)
        e_row = jnp.zeros((8, width), F32)
        starts = []
        for q in range(rows_n):
            starts.append(e)
            e_row = jnp.where(line == q, e, e_row)
            e = down(maps[q], mcoefs[q][0], e)
        l = jnp.zeros((8, width), F32)
        l_row = jnp.zeros((8, width), F32)
        for q in reversed(range(rows_n)):
            l_row = jnp.where(line == q, l, l_row)
            l = up(maps[q], mcoefs[q][1], mcoefs[q][2], starts[q], l)
        e = jnp.where(sub < 3, e_row, pltpu.roll(e_row, 3, 0))
        for t in range(rsize):
            base, of_e, of_l = forms[t]
            ans[k, t] = base + of_e * e + of_l * l_row
        third = {slot: [] for slot in range(3)}
        routes = [(0, gx), (2, west), (1, east)] if k < SECTIONS - 1 else [(0, gx)]
        for slot, column in routes:
            for d in range(1 if slot == 0 else 0, rsize):
                to = lax.rem(place + d, rsize)
                third[slot].append(
                    send(ans.at[k, to], el.at[k, slot, place], s3s.at[k, slot, d], s3r.at[k, slot, d], (column, line0 + to))
                )
        pending.extend(third[0] + third[1] + third[2])
        el[k, 0, place] = ans[k, place]
        if k < SECTIONS - 1:
            plane_copies[0].wait_recv()
            gather_plane(planes.at[k + 1, 1], 1)
        else:
            for copy in trips:
                copy.wait_recv()
            part_out[:, 0:RESIDENT] = moved[0:3, 0:RESIDENT]
            part_out[:, RESIDENT : RESIDENT + CAP] = mig[0, 0:3, :]
            part_out[:, RESIDENT + CAP : RESIDENT + 2 * CAP] = mig[1, 0:3, :] * above_edge
            part_out[:, RESIDENT + 2 * CAP : RESIDENT + 3 * CAP] = mig[2, 0:3, :] * below_edge
        for copy in third[0] + third[2]:
            copy.wait_recv()
        behind = third[1]

    rows = plane_rows(SECTIONS - 1, 0)
    k = SECTIONS - 1
    for c in range(comps):
        field_out[c] = part[k, c] + alpha[k] * rows[c : c + 1] + beta[k] * rows[3 + c : 4 + c]
    for copy in pending:
        copy.wait_send()


def on_device(
    velocity, y_metric, forward_rate, backward_rate, pivot_inv,
    particle_vel, particle_cell, particle_offset, inverse_tau, outgoing_count,
):
    comps, _, cy, cz = velocity.shape
    slots = particle_vel.shape[1]
    nx, lanes = lax.axis_size("gx"), lax.axis_size("gy")
    rsize = row_size(lanes)
    rows_n = lanes // rsize
    width = cz // rsize
    vmem, smem_of = pltpu.VMEM, pltpu.SMEM
    whole = pl.BlockSpec(memory_space=pltpu.VMEM)
    dma = pltpu.SemaphoreType.DMA
    far = pl.BlockSpec(memory_space=pltpu.HBM)

    def stay(x):
        return pltpu.with_memory_space_constraint(x, pltpu.HBM)

    scratch = [
        vmem((comps, cy, cz), F32), vmem((comps, slots), F32), vmem((slots,), jnp.int32),
        vmem((3, slots), F32), vmem((slots,), F32), dma((10,)),
        smem_of((cy,), F32), smem_of((SECTIONS, cy), F32), smem_of((SECTIONS, cy), F32),
        smem_of((SECTIONS, cy), F32), smem_of((3,), jnp.int32),
        vmem((cz, slots), BF16),
        vmem((slots, cz), BF16),
        vmem((4 * comps * cy + 64, cz), BF16),
        vmem((2 * comps * cy, slots), BF16),
        vmem((comps * cy, cz), F32),
        vmem((8, slots), F32),
        vmem((cy, slots), F32),
        vmem((cy, slots), F32),
        vmem((SECTIONS, 8, slots), F32),
        vmem((8, slots), F32),
        vmem((8, slots), F32),
        vmem((1, slots), F32),
        vmem((8, slots), F32),
        vmem((SECTIONS, cy, cy, 128), F32),
        vmem((SECTIONS, cy, 128), F32),
        vmem((SECTIONS, cy, cz), F32),
        vmem((SECTIONS, cy, cz), F32),
        vmem((cy, cz), F32),
        vmem((cy, 128), F32),
        vmem((SECTIONS, comps, cy, cz), F32),
        vmem((SECTIONS, 2, comps, cy, cz), F32),
        vmem((comps, cy, cz), F32),
        vmem((comps, cy, cz), F32),
        vmem((8, cz), F32),
        vmem((3, 8, cz), F32),
        vmem((SECTIONS, rsize, 8, width), F32),
        vmem((SECTIONS, rsize, 8, width), F32),
        vmem((SECTIONS, rows_n, 8, width), F32),
        vmem((SECTIONS, 8, width), F32),
        vmem((SECTIONS, rsize, 8, width), F32),
        vmem((SECTIONS, 3, rsize, 8, width), F32),
        vmem((3, 8, CAP), F32),
        dma((SECTIONS, rsize - 1)), dma((SECTIONS, rsize - 1)),
        dma((SECTIONS, rows_n - 1)), dma((SECTIONS, rows_n - 1)),
        dma((SECTIONS, 3, rsize)), dma((SECTIONS, 3, rsize)),
        dma((SECTIONS, 2)), dma((SECTIONS, 2)),
        dma((3,)), dma((3,)), dma((3,)), dma((3,)),
    ]
    field, moved = pl.pallas_call(
        functools.partial(kernel, (nx, lanes, rsize)),
        out_shape=(
            jax.ShapeDtypeStruct((comps, cy, cz), F32),
            jax.ShapeDtypeStruct((comps, slots), F32),
        ),
        in_specs=[far] * 10,
        out_specs=(whole, whole),
        scratch_shapes=scratch,
        compiler_params=pltpu.CompilerParams(
            collective_id=0, has_side_effects=True, vmem_limit_bytes=48 * 1024 * 1024
        ),
        name="channel_sections",
    )(
        stay(velocity.reshape(comps, cy, cz)),
        stay(y_metric),
        stay(forward_rate),
        stay(backward_rate),
        stay(pivot_inv),
        stay(particle_vel),
        stay(particle_cell),
        stay(particle_offset),
        stay(inverse_tau),
        stay(outgoing_count.reshape(3)),
    )
    return field.reshape(velocity.shape), moved


def solution(mesh):
    return jax.shard_map(
        on_device,
        mesh=mesh,
        in_specs=(
            P(None, "gx", "gy", None),
            P("gy"),
            P(None, "gy"),
            P(None, "gy"),
            P(None, "gy"),
            P(None, ("gx", "gy")),
            P(("gx", "gy")),
            P(None, ("gx", "gy")),
            P(("gx", "gy")),
            P("gx", "gy", None),
        ),
        out_specs=(P(None, "gx", "gy", None), P(None, ("gx", "gy"))),
        check_vma=False,
    )
```

```python
import functools

import jax
import jax.numpy as jnp
from jax import lax
from jax.experimental import pallas as pl
from jax.experimental.pallas import tpu as pltpu
from jax.sharding import PartitionSpec as P

RESIDENT = 2048
CAP = 512
SECTIONS = 3
SECTION_WEIGHTS = (8.0 / 15.0, 5.0 / 12.0, 3.0 / 4.0)
TIME_STEP = 0.3
STREAM_SCALE = 2.0
SPAN_SCALE = 2.0
COUPLING = 0.5
CHUNK = 512
MESH = pl.DeviceIdType.MESH
F32 = jnp.float32
BF16 = jnp.bfloat16


def row_size(lanes):
    return 8 if lanes == 32 else max(2, lanes // 2)


def halves(x):
    high = x.astype(BF16)
    return high, (x - high.astype(F32)).astype(BF16)


def kernel(
    dims,
    vel_in, metric_in, fwd_in, bwd_in, piv_in, pvel_in, cell_in, offset_in, tau_in, count_in,
    field_out, part_out,
    vel, pvel, cell, offset, tau, inputs_sem,
    sm_metric, sm_fwd, sm_bwd, sm_piv, sm_count, onehot, hot_rows, table, scat, accum, wts, ymask, ywt, ab, speed, fluid, live_ref, moved,
    solve_cols, carry_col, alpha, beta, ymet, unit_rows,
    part, planes, uref, rhs_ref, edge, edge_in, msg, got1, got2, own2, ans, el, mig,
    s1s, s1r, s2s, s2r, s3s, s3r, pls, plr, eds, edr, mgs, mgr,
):
    nx, lanes, rsize = dims
    metric, fwd, bwd, piv, count = sm_metric, sm_fwd, sm_bwd, sm_piv, sm_count
    rows_n = lanes // rsize
    comps, cy, cz = vel_in.shape
    width = cz // rsize
    slots = pvel_in.shape[1]
    chunk = min(CHUNK, slots)
    steps = slots // chunk
    last = cy - 1
    rows6 = 2 * comps * cy
    gx = lax.axis_index("gx")
    gy = lax.axis_index("gy")
    place = lax.rem(gy, rsize)
    line = gy // rsize
    line0 = line * rsize
    west = lax.rem(gx + nx - 1, nx)
    east = lax.rem(gx + 1, nx)
    south = lax.rem(gy + lanes - 1, lanes)
    north = lax.rem(gy + 1, lanes)

    def send(src, dst, ssem, rsem, to):
        copy = pltpu.make_async_remote_copy(
            src_ref=src, dst_ref=dst, send_sem=ssem, recv_sem=rsem,
            device_id=to, device_id_type=MESH,
        )
        copy.start()
        return copy

    loads = [
        pltpu.make_async_copy(src, dst, inputs_sem.at[n])
        for n, (src, dst) in enumerate(
            (
                (vel_in, vel), (piv_in, piv), (bwd_in, bwd),
                (cell_in, cell), (offset_in, offset), (pvel_in, pvel), (tau_in, tau),
                (fwd_in, fwd), (metric_in, metric), (count_in, count),
            )
        )
    ]
    partners = []
    for d in range(1, rsize):
        partners.append((gx, line0 + lax.rem(place + d, rsize)))
    for d in range(1, rows_n):
        partners.append((gx, lax.rem(line + d, rows_n) * rsize + place))
    partners += [(west, gy), (east, gy), (gx, south), (gx, north), (west, south), (east, north)]
    barrier = pltpu.get_barrier_semaphore()
    for to in partners:
        pl.semaphore_signal(barrier, inc=1, device_id=to, device_id_type=MESH)

    for load in loads:
        load.start()
    for load in loads[:3]:
        load.wait()
    for c in range(comps):
        edge[c : c + 1, :] = vel[c, last : last + 1, :]
        edge[3 + c : 4 + c, :] = vel[c, 0:1, :]
    edge[6:8, :] = jnp.zeros((2, cz), F32)
    for n, value in enumerate((piv[0, last], bwd[0, last], piv[1, last], bwd[1, last])):
        edge[6:7, n * 128 : (n + 1) * 128] = jnp.full((1, 128), value, F32)

    pl.semaphore_wait(barrier, len(partners))

    pending = []

    def send_planes(k, src):
        a = send(src, planes.at[k, 1], pls.at[k, 0], plr.at[k, 0], (west, gy))
        b = send(src, planes.at[k, 0], pls.at[k, 1], plr.at[k, 1], (east, gy))
        return a, b

    plane_copies = send_planes(0, vel)
    pending.extend(plane_copies)
    edge_copies = [
        send(edge, edge_in.at[0], eds.at[0], edr.at[0], (gx, north)),
        send(edge, edge_in.at[1], eds.at[1], edr.at[1], (gx, south)),
        send(edge, edge_in.at[2], eds.at[2], edr.at[2], (west, south)),
    ]
    pending.extend(edge_copies)

    for load in loads[3:]:
        load.wait()
    row16 = lax.broadcasted_iota(jnp.int32, (cy, chunk), 0)
    lane = lax.broadcasted_iota(jnp.int32, (1, chunk), 1)
    zblock = min(256, cz)
    zrow = lax.broadcasted_iota(jnp.int32, (zblock, chunk), 0).astype(F32).astype(BF16)
    c0, c1, c2 = count[0], count[1], count[2]
    speed[...] = jnp.zeros_like(speed)
    fluid[...] = jnp.zeros_like(fluid)

    def prepare(i, _):
        at = pl.ds(pl.multiple_of(i * chunk, chunk), chunk)
        where = cell[at].reshape(1, chunk)
        zpos = lax.rem(where, cz)
        ypos = lax.rem(lax.div(where, cz), cy)
        for n in range(cz // zblock):
            key = jnp.where(lax.div(zpos, zblock) == n, lax.rem(zpos, zblock), 2 * zblock)
            onehot[n * zblock : (n + 1) * zblock, at] = jnp.where(
                zrow == key.astype(F32).astype(BF16), jnp.bfloat16(1.0), jnp.bfloat16(0.0)
            )
        ox, oy, oz = offset[0:1, at], offset[1:2, at], offset[2:3, at]
        here = row16 == ypos
        above = row16 == ypos + 1
        ymask[:, at] = jnp.where(here, 1.0, 0.0)
        ywt[:, at] = jnp.where(here, 1.0 - oy, jnp.where(above, oy, 0.0))
        wts[0:1, at] = (1.0 - ox) * (1.0 - oz)
        wts[1:2, at] = (1.0 - ox) * oz
        wts[2:3, at] = ox * (1.0 - oz)
        wts[3:4, at] = ox * oz
        wts[4:5, at] = jnp.where(ypos == last, oy, 0.0)
        slot = lane + i * chunk
        out = slot - RESIDENT
        turn = jnp.where(out < CAP, out, jnp.where(out < 2 * CAP, out - CAP, out - 2 * CAP))
        limit = jnp.where(out < CAP, c0, jnp.where(out < 2 * CAP, c1, c2))
        live_ref[:, at] = jnp.where((out < 0) | (turn < limit), 1.0, 0.0)
        speed[0:3, at] = pvel[:, at]
        return 0

    lax.fori_loop(0, steps, prepare, 0)

    lane128 = lax.broadcasted_iota(jnp.int32, (1, 128), 1)

    def rates(k):
        g = jnp.zeros((1, 128), F32)
        gs = []
        for j in range(cy):
            g = jnp.where(lane128 == j, 1.0, 0.0) + fwd[k, j] * g
            gs.append(g)
        u = jnp.zeros((1, 128), F32)
        for j in reversed(range(cy)):
            u = piv[k, j] * gs[j] + bwd[k, j] * u
            unit_rows[j : j + 1, :] = u
        block = unit_rows[...]
        for i in range(cy):
            solve_cols[k, i] = jnp.broadcast_to(block[:, i : i + 1], (cy, 128))
        alpha[k] = jnp.broadcast_to(block[:, 0:1] * fwd[k, 0], (cy, cz))
        weight = jnp.float32(1.0)
        shrink = jnp.float32(1.0)
        for j in reversed(range(cy)):
            carry_col[k, j : j + 1, :] = jnp.full((1, 128), weight, F32)
            weight = weight * fwd[k, j]
            shrink = shrink * bwd[k, j]
            beta[k, j : j + 1, :] = jnp.full((1, cz), shrink, F32)
        for t in range(rsize):
            msg[k, t, 6:7, :] = jnp.full((1, width), weight, F32)
            half = lax.broadcasted_iota(jnp.int32, (1, width), 1) < width // 2
            msg[k, t, 7:8, :] = jnp.where(half, alpha[k, 0:1, 0:width], shrink)

    rates(0)
    for j in range(cy):
        ymet[j : j + 1, :] = jnp.full((1, cz), 0.5 * metric[j], F32)

    def responses(k):
        two = jnp.zeros((2, chunk), F32)
        for i in range(steps):
            at = slice(i * chunk, (i + 1) * chunk)
            top = wts[4:5, at]
            if k == 0:
                a, b = jnp.zeros((1, chunk), F32), top
            else:
                w = ywt[:, at]
                a = jnp.sum(w * alpha[k - 1, :, 0:1], axis=0, keepdims=True)
                b = jnp.sum(w * beta[k - 1, :, 0:1], axis=0, keepdims=True) + top
            ab[:, at] = jnp.concatenate([a, a, a, b, b, b, two], axis=0)

    def fill_table(source):
        for c in range(comps):
            x = source[c]
            high, low = halves(x)
            table[c * cy : (c + 1) * cy, :] = high
            table[rows6 + c * cy : rows6 + (c + 1) * cy, :] = low
            high, low = halves(pltpu.roll(x, cz - 1, 1))
            at = (comps + c) * cy
            table[at : at + cy, :] = high
            table[rows6 + at : rows6 + at + cy, :] = low

    def interpolate(got, side, at):
        got = got[0:rows6] + got[rows6 : 2 * rows6]
        w0 = wts[2 * side : 2 * side + 1, at]
        w1 = wts[2 * side + 1 : 2 * side + 2, at]
        w = ywt[:, at]
        rows = []
        for c in range(comps):
            near = got[c * cy : (c + 1) * cy]
            far = got[(comps + c) * cy : (comps + c + 1) * cy]
            rows.append(jnp.sum((w0 * near + w1 * far) * w, axis=0, keepdims=True))
        value = jnp.concatenate(rows, axis=0)
        if side == 0:
            fluid[0:3, at] = value
        else:
            fluid[0:3, at] = fluid[0:3, at] + value

    def gather_plane(source, side):
        fill_table(source)
        for i in range(steps):
            at = slice(i * chunk, (i + 1) * chunk)
            got = jnp.dot(table[0 : 2 * rows6, :], onehot[:, at], preferred_element_type=F32)
            interpolate(got, side, at)

    sub = lax.broadcasted_iota(jnp.int32, (8, width), 0)
    col = lax.broadcasted_iota(jnp.int32, (8, width), 1)

    def coefficients(x):
        grow = jnp.broadcast_to(x[6:7], (8, width))
        seven = jnp.broadcast_to(x[7:8], (8, width))
        other = pltpu.roll(seven, width // 2, 1)
        mixed = jnp.where(col < width // 2, seven, other)
        shrink = jnp.where(col < width // 2, other, seven)
        return grow, mixed, shrink

    def lifted(e):
        return jnp.where((sub >= 3) & (sub < 6), pltpu.roll(e, 3, 0), jnp.where(sub == 6, e, 0.0))

    def down(x, grow, e):
        return jnp.where(sub < 3, x, 0.0) + grow * e

    def up(x, mixed, shrink, e, l):
        return jnp.where((sub >= 3) & (sub < 6), x, 0.0) + mixed * lifted(e) + shrink * l

    def plane_rows(k, slot):
        return jnp.concatenate([el[k, slot, t] for t in range(rsize)], axis=1)

    below_edge = jnp.where(gy > 0, 1.0, 0.0).astype(F32)
    above_edge = jnp.where(gy < lanes - 1, 1.0, 0.0).astype(F32)

    gather_plane(vel, 0)
    responses(0)
    wide = lax.broadcasted_iota(jnp.int32, (128, cz), 1)
    for n in range(slots // 128):
        zpos = lax.rem(cell[n * 128 : (n + 1) * 128].reshape(1, 128), cz)
        column = jnp.transpose(jnp.broadcast_to(zpos.astype(F32), (128, 128))).astype(jnp.int32)
        spread = jnp.concatenate([column] * (cz // 128), axis=1)
        hot_rows[n * 128 : (n + 1) * 128, :] = jnp.where(wide == spread, 1.0, 0.0).astype(BF16)
    for copy in edge_copies:
        copy.wait_recv()
    plane_copies[0].wait_recv()
    fill_table(planes.at[0, 1])
    behind = []

    for k in range(SECTIONS):
        step = TIME_STEP * SECTION_WEIGHTS[k]
        if k == 0:
            sub_full = lax.broadcasted_iota(jnp.int32, (8, cz), 0)
            upper = jnp.where((sub_full >= 3) & (sub_full < 6), 1.0, 0.0) * above_edge
            lower = jnp.where(sub_full < 3, 1.0, 0.0) * below_edge
            own = edge_in[0] * lower + edge_in[1] * upper
            plus = edge_in[2] * upper
        else:
            own, plus = plane_rows(k - 1, 0), plane_rows(k - 1, 2)
        pair = jnp.concatenate([own, plus], axis=0)
        high, low = halves(pair)
        table[2 * rows6 + 0 : 2 * rows6 + 16, :] = high
        table[2 * rows6 + 32 : 2 * rows6 + 48, :] = low
        high, low = halves(pltpu.roll(pair, cz - 1, 1))
        table[2 * rows6 + 16 : 2 * rows6 + 32, :] = high
        table[2 * rows6 + 48 : 2 * rows6 + 64, :] = low

        def push(i, k=k, step=step):
            at = slice(i * chunk, (i + 1) * chunk)
            hot = onehot[:, at]
            base = 2 * rows6 if k else 0
            got = jnp.dot(table[base:, :], hot, preferred_element_type=F32)
            if k == 0:
                interpolate(got, 1, at)
                got = got[2 * rows6 :]
            got = got[0:32] + got[32:64]
            mix = (
                wts[0:1, at] * got[0:8]
                + wts[2:3, at] * got[8:16]
                + wts[1:2, at] * got[16:24]
                + wts[3:4, at] * got[24:32]
            ) * ab[:, at]
            flow = fluid[:, at] + mix + pltpu.roll(mix, 5, 0)
            now = speed[:, at]
            drag = tau[at].reshape(1, chunk) * (flow - now)
            speed[:, at] = now + step * drag
            share = drag * (-COUPLING * live_ref[:, at])
            mask = ymask[:, at]
            for c in range(comps):
                one = share[c : c + 1]
                head = one.astype(BF16).astype(F32)
                scat[c * cy : (c + 1) * cy, at] = (mask * head).astype(BF16)
                scat[(comps + c) * cy : (comps + c + 1) * cy, at] = (mask * (one - head)).astype(BF16)

        for i in range(steps):
            push(i)

        if k == SECTIONS - 1:
            moved[...] = speed[...] * live_ref[...]
            trips = [
                send(moved.at[:, RESIDENT : RESIDENT + CAP], mig.at[0], mgs.at[0], mgr.at[0], (east, gy)),
                send(moved.at[:, RESIDENT + CAP : RESIDENT + 2 * CAP], mig.at[1], mgs.at[1], mgr.at[1], (gx, south)),
                send(moved.at[:, RESIDENT + 2 * CAP : RESIDENT + 3 * CAP], mig.at[2], mgs.at[2], mgr.at[2], (gx, north)),
            ]
            pending.extend(trips)

        plane_copies[1].wait_recv()
        for copy in behind:
            copy.wait_recv()
        minus = plane_rows(k - 1, 1) if k > 0 else None

        def gathered(n):
            at = slice(n * zblock, (n + 1) * zblock)
            both = lax.dot_general(
                scat[...], hot_rows[:, at], (((1,), (0,)), ((), ())), preferred_element_type=F32
            )
            half = comps * cy
            accum[:, at] = both[0:half] + both[half : 2 * half]

        for n in range(cz // zblock):
            gathered(n)

        def plane(source, c, rows):
            if k == 0:
                return source[c]
            return source[c] + alpha[k - 1] * rows[c : c + 1] + beta[k - 1] * rows[3 + c : 4 + c]

        for c in range(comps):
            uref[c] = plane(vel if k == 0 else part.at[k - 1], c, own)
        rowz = lax.broadcasted_iota(jnp.int32, (cy, cz), 0)
        for c in range(comps):
            u = uref[c]
            slope_x = (plane(planes.at[k, 1], c, plus) - plane(planes.at[k, 0], c, minus)) * (
                0.5 * STREAM_SCALE
            )
            slope_z = (pltpu.roll(u, cz - 1, 1) - pltpu.roll(u, 1, 1)) * (0.5 * SPAN_SCALE)
            if k == 0:
                under = own[c : c + 1]
            else:
                rate = edge_in[0, 6:7, :]
                base = 256 * (k - 1)
                pv = jnp.concatenate([rate[:, base : base + 128]] * (cz // 128), axis=1)
                bv = jnp.concatenate([rate[:, base + 128 : base + 256]] * (cz // 128), axis=1)
                under = (pv * own[c : c + 1] + bv * u[0:1]) * below_edge
            upper_y = jnp.where(rowz == last, own[3 + c : 4 + c], pltpu.roll(u, cy - 1, 0))
            lower_y = jnp.where(rowz == 0, under, pltpu.roll(u, 1, 0))
            slope_y = (upper_y - lower_y) * ymet[...]
            convection = -(uref[0] * slope_x + uref[1] * slope_y + uref[2] * slope_z)
            rhs_ref[c] = u + step * (convection + accum[c * cy : (c + 1) * cy, :])

        for c in range(comps):
            for z in range(cz // 128):
                at = slice(z * 128, (z + 1) * 128)
                total = None
                for i in range(cy):
                    term = solve_cols[k, i] * rhs_ref[c, i : i + 1, at]
                    total = term if total is None else total + term
                part[k, c, :, at] = total
                leave = jnp.sum(carry_col[k] * rhs_ref[c, :, at], axis=0, keepdims=True)
                t, o = (z * 128) // width, (z * 128) % width
                msg[k, t, c : c + 1, o : o + 128] = leave
                msg[k, t, 3 + c : 4 + c, o : o + 128] = total[0:1]

        if k == SECTIONS - 1:
            sent, pending = pending, []
        first = []
        for d in range(1, rsize):
            to = lax.rem(place + d, rsize)
            first.append(
                send(msg.at[k, to], got1.at[k, place], s1s.at[k, d - 1], s1r.at[k, d - 1], (gx, line0 + to))
            )
        pending.extend(first)
        got1[k, place] = msg[k, place]
        if k < SECTIONS - 1:
            plane_copies = send_planes(k + 1, part.at[k])
            pending.extend(plane_copies)
            gather_plane(part.at[k], 0)
        for copy in first:
            copy.wait_recv()
        tiles = [got1[k, t] for t in range(rsize)]
        coefs = [coefficients(x) for x in tiles]
        e = jnp.where(sub == 6, 1.0, 0.0)
        starts = []
        for t in range(rsize):
            starts.append(e)
            e = down(tiles[t], coefs[t][0], e)
        l = jnp.where(sub == 7, 1.0, 0.0)
        ends = [None] * rsize
        for t in reversed(range(rsize)):
            ends[t] = l
            l = up(tiles[t], coefs[t][1], coefs[t][2], starts[t], l)
        whole = jnp.where(
            (sub < 3) | (sub == 6),
            e,
            jnp.where((sub == 7) & (col < width // 2), pltpu.roll(l, 1, 0), l),
        )
        own2[k] = whole
        got2[k, line] = whole
        second = []
        for d in range(1, rows_n):
            to = lax.rem(line + d, rows_n)
            second.append(
                send(own2.at[k], got2.at[k, line], s2s.at[k, d - 1], s2r.at[k, d - 1], (gx, to * rsize + place))
            )
        pending.extend(second)
        middle = (sub >= 3) & (sub < 6)
        forms = []
        for t in range(rsize):
            base = jnp.where(sub < 3, starts[t], jnp.where(middle, ends[t], 0.0))
            of_e = jnp.where(sub < 3, starts[t][6:7], jnp.where(middle, ends[t][6:7], 0.0))
            of_l = jnp.where(middle, ends[t][7:8], 0.0)
            forms.append((base, of_e, of_l))
        if k < SECTIONS - 1:
            rates(k + 1)
            responses(k + 1)
        else:
            while sent:
                sent.pop().wait_send()
        for copy in second:
            copy.wait_recv()
        maps = [got2[k, q] for q in range(rows_n)]
        mcoefs = [coefficients(x) for x in maps]
        e = jnp.zeros((8, width), F32)
        e_row = jnp.zeros((8, width), F32)
        starts = []
        for q in range(rows_n):
            starts.append(e)
            e_row = jnp.where(line == q, e, e_row)
            e = down(maps[q], mcoefs[q][0], e)
        l = jnp.zeros((8, width), F32)
        l_row = jnp.zeros((8, width), F32)
        for q in reversed(range(rows_n)):
            l_row = jnp.where(line == q, l, l_row)
            l = up(maps[q], mcoefs[q][1], mcoefs[q][2], starts[q], l)
        e = jnp.where(sub < 3, e_row, pltpu.roll(e_row, 3, 0))
        for t in range(rsize):
            base, of_e, of_l = forms[t]
            ans[k, t] = base + of_e * e + of_l * l_row
        third = {slot: [] for slot in range(3)}
        routes = [(0, gx), (2, west), (1, east)] if k < SECTIONS - 1 else [(0, gx)]
        for slot, column in routes:
            for d in range(1 if slot == 0 else 0, rsize):
                to = lax.rem(place + d, rsize)
                third[slot].append(
                    send(ans.at[k, to], el.at[k, slot, place], s3s.at[k, slot, d], s3r.at[k, slot, d], (column, line0 + to))
                )
        pending.extend(third[0] + third[1] + third[2])
        el[k, 0, place] = ans[k, place]
        if k < SECTIONS - 1:
            plane_copies[0].wait_recv()
            gather_plane(planes.at[k + 1, 1], 1)
        else:
            for copy in trips:
                copy.wait_recv()
            part_out[:, 0:RESIDENT] = moved[0:3, 0:RESIDENT]
            part_out[:, RESIDENT : RESIDENT + CAP] = mig[0, 0:3, :]
            part_out[:, RESIDENT + CAP : RESIDENT + 2 * CAP] = mig[1, 0:3, :] * above_edge
            part_out[:, RESIDENT + 2 * CAP : RESIDENT + 3 * CAP] = mig[2, 0:3, :] * below_edge
        for copy in third[0] + third[2]:
            copy.wait_recv()
        behind = third[1]

    rows = plane_rows(SECTIONS - 1, 0)
    k = SECTIONS - 1
    for c in range(comps):
        field_out[c] = part[k, c] + alpha[k] * rows[c : c + 1] + beta[k] * rows[3 + c : 4 + c]
    for copy in pending:
        copy.wait_send()


def finish(field, moved, field_out, moved_out, sems):
    copies = [
        pltpu.make_async_copy(field, field_out, sems.at[0]),
        pltpu.make_async_copy(moved, moved_out, sems.at[1]),
    ]
    for copy in copies:
        copy.start()
    for copy in copies:
        copy.wait()


def on_device(
    velocity, y_metric, forward_rate, backward_rate, pivot_inv,
    particle_vel, particle_cell, particle_offset, inverse_tau, outgoing_count,
):
    comps, _, cy, cz = velocity.shape
    slots = particle_vel.shape[1]
    nx, lanes = lax.axis_size("gx"), lax.axis_size("gy")
    rsize = row_size(lanes)
    rows_n = lanes // rsize
    width = cz // rsize
    vmem, smem_of = pltpu.VMEM, pltpu.SMEM
    whole = pl.BlockSpec(memory_space=pltpu.VMEM)
    dma = pltpu.SemaphoreType.DMA
    far = pl.BlockSpec(memory_space=pltpu.HBM)

    def stay(x):
        return pltpu.with_memory_space_constraint(x, pltpu.HBM)

    scratch = [
        vmem((comps, cy, cz), F32), vmem((comps, slots), F32), vmem((slots,), jnp.int32),
        vmem((3, slots), F32), vmem((slots,), F32), dma((10,)),
        smem_of((cy,), F32), smem_of((SECTIONS, cy), F32), smem_of((SECTIONS, cy), F32),
        smem_of((SECTIONS, cy), F32), smem_of((3,), jnp.int32),
        vmem((cz, slots), BF16),
        vmem((slots, cz), BF16),
        vmem((4 * comps * cy + 64, cz), BF16),
        vmem((2 * comps * cy, slots), BF16),
        vmem((comps * cy, cz), F32),
        vmem((8, slots), F32),
        vmem((cy, slots), F32),
        vmem((cy, slots), F32),
        vmem((8, slots), F32),
        vmem((8, slots), F32),
        vmem((8, slots), F32),
        vmem((1, slots), F32),
        vmem((8, slots), F32),
        vmem((SECTIONS, cy, cy, 128), F32),
        vmem((SECTIONS, cy, 128), F32),
        vmem((SECTIONS, cy, cz), F32),
        vmem((SECTIONS, cy, cz), F32),
        vmem((cy, cz), F32),
        vmem((cy, 128), F32),
        vmem((SECTIONS, comps, cy, cz), F32),
        vmem((SECTIONS, 2, comps, cy, cz), F32),
        vmem((comps, cy, cz), F32),
        vmem((comps, cy, cz), F32),
        vmem((8, cz), F32),
        vmem((3, 8, cz), F32),
        vmem((SECTIONS, rsize, 8, width), F32),
        vmem((SECTIONS, rsize, 8, width), F32),
        vmem((SECTIONS, rows_n, 8, width), F32),
        vmem((SECTIONS, 8, width), F32),
        vmem((SECTIONS, rsize, 8, width), F32),
        vmem((SECTIONS, 3, rsize, 8, width), F32),
        vmem((3, 8, CAP), F32),
        dma((SECTIONS, rsize - 1)), dma((SECTIONS, rsize - 1)),
        dma((SECTIONS, rows_n - 1)), dma((SECTIONS, rows_n - 1)),
        dma((SECTIONS, 3, rsize)), dma((SECTIONS, 3, rsize)),
        dma((SECTIONS, 2)), dma((SECTIONS, 2)),
        dma((3,)), dma((3,)), dma((3,)), dma((3,)),
    ]
    field, moved = pl.pallas_call(
        functools.partial(kernel, (nx, lanes, rsize)),
        out_shape=(
            jax.ShapeDtypeStruct((comps, cy, cz), F32),
            jax.ShapeDtypeStruct((comps, slots), F32),
        ),
        in_specs=[far] * 10,
        out_specs=(whole, whole),
        scratch_shapes=scratch,
        compiler_params=pltpu.CompilerParams(
            collective_id=0, has_side_effects=True, vmem_limit_bytes=48 * 1024 * 1024
        ),
        name="channel_sections",
    )(
        stay(velocity.reshape(comps, cy, cz)),
        stay(y_metric),
        stay(forward_rate),
        stay(backward_rate),
        stay(pivot_inv),
        stay(particle_vel),
        stay(particle_cell),
        stay(particle_offset),
        stay(inverse_tau),
        stay(outgoing_count.reshape(3)),
    )
    field, moved = pl.pallas_call(
        finish,
        out_shape=(
            jax.ShapeDtypeStruct((comps, cy, cz), F32),
            jax.ShapeDtypeStruct((comps, slots), F32),
        ),
        in_specs=[whole, whole],
        out_specs=(far, far),
        scratch_shapes=[dma((2,))],
        compiler_params=pltpu.CompilerParams(vmem_limit_bytes=4 * 1024 * 1024),
        name="write_out",
    )(field, moved)
    return field.reshape(velocity.shape), moved


def solution(mesh):
    return jax.shard_map(
        on_device,
        mesh=mesh,
        in_specs=(
            P(None, "gx", "gy", None),
            P("gy"),
            P(None, "gy"),
            P(None, "gy"),
            P(None, "gy"),
            P(None, ("gx", "gy")),
            P(("gx", "gy")),
            P(None, ("gx", "gy")),
            P(("gx", "gy")),
            P("gx", "gy", None),
        ),
        out_specs=(P(None, "gx", "gy", None), P(None, ("gx", "gy"))),
        check_vma=False,
    )
```

```python
import functools

import jax
import jax.numpy as jnp
from jax import lax
from jax.experimental import pallas as pl
from jax.experimental.pallas import tpu as pltpu
from jax.sharding import PartitionSpec as P

RESIDENT = 2048
CAP = 512
SECTIONS = 3
SECTION_WEIGHTS = (8.0 / 15.0, 5.0 / 12.0, 3.0 / 4.0)
TIME_STEP = 0.3
STREAM_SCALE = 2.0
SPAN_SCALE = 2.0
COUPLING = 0.5
CHUNK = 512
MESH = pl.DeviceIdType.MESH
F32 = jnp.float32
BF16 = jnp.bfloat16


def row_size(lanes):
    return 8 if lanes == 32 else max(2, lanes // 2)


def halves(x):
    high = x.astype(BF16)
    return high, (x - high.astype(F32)).astype(BF16)


def thirds(x):
    high = x.astype(BF16)
    rest = x - high.astype(F32)
    low = rest.astype(BF16)
    return high, low, (rest - low.astype(F32)).astype(BF16)


def kernel(
    dims,
    vel_in, metric_in, fwd_in, bwd_in, piv_in, pvel_in, cell_in, offset_in, tau_in, count_in,
    field_out, part_out,
    vel, pvel, cell, offset, tau, inputs_sem,
    sm_metric, sm_fwd, sm_bwd, sm_piv, sm_count, onehot, hot_rows, table, scat, accum, wts, ymask, ywt, ab, speed, fluid, live_ref, moved,
    solve_mat, stacked, alpha, beta, ymet, unit_rows,
    part, planes, uref, edge, edge_in, msg, got1, got2, own2, ans, el, mig,
    s1s, s1r, s2s, s2r, s3s, s3r, pls, plr, eds, edr, mgs, mgr,
):
    nx, lanes, rsize = dims
    metric, fwd, bwd, piv, count = sm_metric, sm_fwd, sm_bwd, sm_piv, sm_count
    rows_n = lanes // rsize
    comps, cy, cz = vel_in.shape
    width = cz // rsize
    slots = pvel_in.shape[1]
    chunk = min(CHUNK, slots)
    steps = slots // chunk
    last = cy - 1
    rows6 = 2 * comps * cy
    gx = lax.axis_index("gx")
    gy = lax.axis_index("gy")
    place = lax.rem(gy, rsize)
    line = gy // rsize
    line0 = line * rsize
    west = lax.rem(gx + nx - 1, nx)
    east = lax.rem(gx + 1, nx)
    south = lax.rem(gy + lanes - 1, lanes)
    north = lax.rem(gy + 1, lanes)

    def send(src, dst, ssem, rsem, to):
        copy = pltpu.make_async_remote_copy(
            src_ref=src, dst_ref=dst, send_sem=ssem, recv_sem=rsem,
            device_id=to, device_id_type=MESH,
        )
        copy.start()
        return copy

    loads = [
        pltpu.make_async_copy(src, dst, inputs_sem.at[n])
        for n, (src, dst) in enumerate(
            (
                (vel_in, vel), (piv_in, piv), (bwd_in, bwd),
                (cell_in, cell), (offset_in, offset), (pvel_in, pvel), (tau_in, tau),
                (fwd_in, fwd), (metric_in, metric), (count_in, count),
            )
        )
    ]
    partners = []
    for d in range(1, rsize):
        partners.append((gx, line0 + lax.rem(place + d, rsize)))
    for d in range(1, rows_n):
        partners.append((gx, lax.rem(line + d, rows_n) * rsize + place))
    partners += [(west, gy), (east, gy), (gx, south), (gx, north), (west, south), (east, north)]
    barrier = pltpu.get_barrier_semaphore()
    for to in partners:
        pl.semaphore_signal(barrier, inc=1, device_id=to, device_id_type=MESH)

    for load in loads:
        load.start()
    for load in loads[:3]:
        load.wait()
    for c in range(comps):
        edge[c : c + 1, :] = vel[c, last : last + 1, :]
        edge[3 + c : 4 + c, :] = vel[c, 0:1, :]
    edge[6:8, :] = jnp.zeros((2, cz), F32)
    for n, value in enumerate((piv[0, last], bwd[0, last], piv[1, last], bwd[1, last])):
        edge[6:7, n * 128 : (n + 1) * 128] = jnp.full((1, 128), value, F32)

    pl.semaphore_wait(barrier, len(partners))

    pending = []

    def send_planes(k, src):
        a = send(src, planes.at[k, 1], pls.at[k, 0], plr.at[k, 0], (west, gy))
        b = send(src, planes.at[k, 0], pls.at[k, 1], plr.at[k, 1], (east, gy))
        return a, b

    plane_copies = send_planes(0, vel)
    pending.extend(plane_copies)
    edge_copies = [
        send(edge, edge_in.at[0], eds.at[0], edr.at[0], (gx, north)),
        send(edge, edge_in.at[1], eds.at[1], edr.at[1], (gx, south)),
        send(edge, edge_in.at[2], eds.at[2], edr.at[2], (west, south)),
    ]
    pending.extend(edge_copies)

    for load in loads[3:]:
        load.wait()
    row16 = lax.broadcasted_iota(jnp.int32, (cy, chunk), 0)
    lane = lax.broadcasted_iota(jnp.int32, (1, chunk), 1)
    zblock = min(256, cz)
    zrow = lax.broadcasted_iota(jnp.int32, (zblock, chunk), 0).astype(F32).astype(BF16)
    c0, c1, c2 = count[0], count[1], count[2]
    speed[...] = jnp.zeros_like(speed)
    fluid[...] = jnp.zeros_like(fluid)
    stacked[...] = jnp.zeros_like(stacked)

    def prepare(i, _):
        at = pl.ds(pl.multiple_of(i * chunk, chunk), chunk)
        where = cell[at].reshape(1, chunk)
        zpos = lax.rem(where, cz)
        ypos = lax.rem(lax.div(where, cz), cy)
        for n in range(cz // zblock):
            key = jnp.where(lax.div(zpos, zblock) == n, lax.rem(zpos, zblock), 2 * zblock)
            onehot[n * zblock : (n + 1) * zblock, at] = jnp.where(
                zrow == key.astype(F32).astype(BF16), jnp.bfloat16(1.0), jnp.bfloat16(0.0)
            )
        ox, oy, oz = offset[0:1, at], offset[1:2, at], offset[2:3, at]
        here = row16 == ypos
        above = row16 == ypos + 1
        ymask[:, at] = jnp.where(here, 1.0, 0.0)
        ywt[:, at] = jnp.where(here, 1.0 - oy, jnp.where(above, oy, 0.0))
        wts[0:1, at] = (1.0 - ox) * (1.0 - oz)
        wts[1:2, at] = (1.0 - ox) * oz
        wts[2:3, at] = ox * (1.0 - oz)
        wts[3:4, at] = ox * oz
        wts[4:5, at] = jnp.where(ypos == last, oy, 0.0)
        slot = lane + i * chunk
        out = slot - RESIDENT
        turn = jnp.where(out < CAP, out, jnp.where(out < 2 * CAP, out - CAP, out - 2 * CAP))
        limit = jnp.where(out < CAP, c0, jnp.where(out < 2 * CAP, c1, c2))
        live_ref[:, at] = jnp.where((out < 0) | (turn < limit), 1.0, 0.0)
        speed[0:3, at] = pvel[:, at]
        return 0

    lax.fori_loop(0, steps, prepare, 0)

    lane128 = lax.broadcasted_iota(jnp.int32, (1, 128), 1)

    def rates(k):
        g = jnp.zeros((1, 128), F32)
        gs = []
        for j in range(cy):
            g = jnp.where(lane128 == j, 1.0, 0.0) + fwd[k, j] * g
            gs.append(g)
        u = jnp.zeros((1, 128), F32)
        for j in reversed(range(cy)):
            u = piv[k, j] * gs[j] + bwd[k, j] * u
            unit_rows[j : j + 1, :] = u
        block = unit_rows[...]
        full = jnp.concatenate([block, gs[last], jnp.zeros((cy - 1, 128), F32)], axis=0)
        pa, pb, pc = (x.astype(F32) for x in thirds(full))
        total = pa
        for n, x in enumerate((pa, pa, pb, pb, pc)):
            total = total + pltpu.roll(x, (n + 1) * cy, 1)
        solve_mat[k] = total.astype(BF16)
        alpha[k] = jnp.broadcast_to(block[:, 0:1] * fwd[k, 0], (cy, cz))
        weight = jnp.float32(1.0)
        shrink = jnp.float32(1.0)
        for j in reversed(range(cy)):
            weight = weight * fwd[k, j]
            shrink = shrink * bwd[k, j]
            beta[k, j : j + 1, :] = jnp.full((1, cz), shrink, F32)
        for t in range(rsize):
            msg[k, t, 6:7, :] = jnp.full((1, width), weight, F32)
            half = lax.broadcasted_iota(jnp.int32, (1, width), 1) < width // 2
            msg[k, t, 7:8, :] = jnp.where(half, alpha[k, 0:1, 0:width], shrink)

    rates(0)
    for j in range(cy):
        ymet[j : j + 1, :] = jnp.full((1, cz), 0.5 * metric[j], F32)

    def responses(k):
        two = jnp.zeros((2, chunk), F32)
        for i in range(steps):
            at = slice(i * chunk, (i + 1) * chunk)
            top = wts[4:5, at]
            if k == 0:
                a, b = jnp.zeros((1, chunk), F32), top
            else:
                w = ywt[:, at]
                a = jnp.sum(w * alpha[k - 1, :, 0:1], axis=0, keepdims=True)
                b = jnp.sum(w * beta[k - 1, :, 0:1], axis=0, keepdims=True) + top
            ab[:, at] = jnp.concatenate([a, a, a, b, b, b, two], axis=0)

    def fill_table(source):
        for c in range(comps):
            x = source[c]
            high, low = halves(x)
            table[c * cy : (c + 1) * cy, :] = high
            table[rows6 + c * cy : rows6 + (c + 1) * cy, :] = low
            high, low = halves(pltpu.roll(x, cz - 1, 1))
            at = (comps + c) * cy
            table[at : at + cy, :] = high
            table[rows6 + at : rows6 + at + cy, :] = low

    def interpolate(got, side, at):
        got = got[0:rows6] + got[rows6 : 2 * rows6]
        w0 = wts[2 * side : 2 * side + 1, at]
        w1 = wts[2 * side + 1 : 2 * side + 2, at]
        w = ywt[:, at]
        rows = []
        for c in range(comps):
            near = got[c * cy : (c + 1) * cy]
            far = got[(comps + c) * cy : (comps + c + 1) * cy]
            rows.append(jnp.sum((w0 * near + w1 * far) * w, axis=0, keepdims=True))
        value = jnp.concatenate(rows, axis=0)
        if side == 0:
            fluid[0:3, at] = value
        else:
            fluid[0:3, at] = fluid[0:3, at] + value

    def gather_plane(source, side):
        fill_table(source)
        for i in range(steps):
            at = slice(i * chunk, (i + 1) * chunk)
            got = jnp.dot(table[0 : 2 * rows6, :], onehot[:, at], preferred_element_type=F32)
            interpolate(got, side, at)

    sub = lax.broadcasted_iota(jnp.int32, (8, width), 0)
    col = lax.broadcasted_iota(jnp.int32, (8, width), 1)

    def coefficients(x):
        grow = jnp.broadcast_to(x[6:7], (8, width))
        seven = jnp.broadcast_to(x[7:8], (8, width))
        other = pltpu.roll(seven, width // 2, 1)
        mixed = jnp.where(col < width // 2, seven, other)
        shrink = jnp.where(col < width // 2, other, seven)
        return grow, mixed, shrink

    def lifted(e):
        return jnp.where((sub >= 3) & (sub < 6), pltpu.roll(e, 3, 0), jnp.where(sub == 6, e, 0.0))

    def down(x, grow, e):
        return jnp.where(sub < 3, x, 0.0) + grow * e

    def up(x, mixed, shrink, e, l):
        return jnp.where((sub >= 3) & (sub < 6), x, 0.0) + mixed * lifted(e) + shrink * l

    def plane_rows(k, slot):
        return jnp.concatenate([el[k, slot, t] for t in range(rsize)], axis=1)

    below_edge = jnp.where(gy > 0, 1.0, 0.0).astype(F32)
    above_edge = jnp.where(gy < lanes - 1, 1.0, 0.0).astype(F32)

    gather_plane(vel, 0)
    responses(0)
    wide = lax.broadcasted_iota(jnp.int32, (128, cz), 1)
    for n in range(slots // 128):
        zpos = lax.rem(cell[n * 128 : (n + 1) * 128].reshape(1, 128), cz)
        column = jnp.transpose(jnp.broadcast_to(zpos.astype(F32), (128, 128))).astype(jnp.int32)
        spread = jnp.concatenate([column] * (cz // 128), axis=1)
        hot_rows[n * 128 : (n + 1) * 128, :] = jnp.where(wide == spread, 1.0, 0.0).astype(BF16)
    for copy in edge_copies:
        copy.wait_recv()
    plane_copies[0].wait_recv()
    fill_table(planes.at[0, 1])
    behind = []

    for k in range(SECTIONS):
        step = TIME_STEP * SECTION_WEIGHTS[k]
        if k == 0:
            sub_full = lax.broadcasted_iota(jnp.int32, (8, cz), 0)
            upper = jnp.where((sub_full >= 3) & (sub_full < 6), 1.0, 0.0) * above_edge
            lower = jnp.where(sub_full < 3, 1.0, 0.0) * below_edge
            own = edge_in[0] * lower + edge_in[1] * upper
            plus = edge_in[2] * upper
        else:
            own, plus = plane_rows(k - 1, 0), plane_rows(k - 1, 2)
        pair = jnp.concatenate([own, plus], axis=0)
        high, low = halves(pair)
        table[2 * rows6 + 0 : 2 * rows6 + 16, :] = high
        table[2 * rows6 + 32 : 2 * rows6 + 48, :] = low
        high, low = halves(pltpu.roll(pair, cz - 1, 1))
        table[2 * rows6 + 16 : 2 * rows6 + 32, :] = high
        table[2 * rows6 + 48 : 2 * rows6 + 64, :] = low

        def push(i, k=k, step=step):
            at = slice(i * chunk, (i + 1) * chunk)
            hot = onehot[:, at]
            base = 2 * rows6 if k else 0
            got = jnp.dot(table[base:, :], hot, preferred_element_type=F32)
            if k == 0:
                interpolate(got, 1, at)
                got = got[2 * rows6 :]
            got = got[0:32] + got[32:64]
            mix = (
                wts[0:1, at] * got[0:8]
                + wts[2:3, at] * got[8:16]
                + wts[1:2, at] * got[16:24]
                + wts[3:4, at] * got[24:32]
            ) * ab[:, at]
            flow = fluid[:, at] + mix + pltpu.roll(mix, 5, 0)
            now = speed[:, at]
            drag = tau[at].reshape(1, chunk) * (flow - now)
            speed[:, at] = now + step * drag
            share = drag * (-COUPLING * live_ref[:, at])
            mask = ymask[:, at]
            for c in range(comps):
                one = share[c : c + 1]
                head = one.astype(BF16).astype(F32)
                scat[c * cy : (c + 1) * cy, at] = (mask * head).astype(BF16)
                scat[(comps + c) * cy : (comps + c + 1) * cy, at] = (mask * (one - head)).astype(BF16)

        for i in range(steps):
            push(i)

        if k == SECTIONS - 1:
            moved[...] = speed[...] * live_ref[...]
            trips = [
                send(moved.at[:, RESIDENT : RESIDENT + CAP], mig.at[0], mgs.at[0], mgr.at[0], (east, gy)),
                send(moved.at[:, RESIDENT + CAP : RESIDENT + 2 * CAP], mig.at[1], mgs.at[1], mgr.at[1], (gx, south)),
                send(moved.at[:, RESIDENT + 2 * CAP : RESIDENT + 3 * CAP], mig.at[2], mgs.at[2], mgr.at[2], (gx, north)),
            ]
            pending.extend(trips)

        plane_copies[1].wait_recv()
        for copy in behind:
            copy.wait_recv()
        minus = plane_rows(k - 1, 1) if k > 0 else None

        def gathered(n):
            at = slice(n * zblock, (n + 1) * zblock)
            both = lax.dot_general(
                scat[...], hot_rows[:, at], (((1,), (0,)), ((), ())), preferred_element_type=F32
            )
            half = comps * cy
            accum[:, at] = both[0:half] + both[half : 2 * half]

        for n in range(cz // zblock):
            gathered(n)

        def plane(source, c, rows):
            if k == 0:
                return source[c]
            return source[c] + alpha[k - 1] * rows[c : c + 1] + beta[k - 1] * rows[3 + c : 4 + c]

        for c in range(comps):
            uref[c] = plane(vel if k == 0 else part.at[k - 1], c, own)
        rowz = lax.broadcasted_iota(jnp.int32, (cy, cz), 0)
        for c in range(comps):
            u = uref[c]
            slope_x = (plane(planes.at[k, 1], c, plus) - plane(planes.at[k, 0], c, minus)) * (
                0.5 * STREAM_SCALE
            )
            slope_z = (pltpu.roll(u, cz - 1, 1) - pltpu.roll(u, 1, 1)) * (0.5 * SPAN_SCALE)
            if k == 0:
                under = own[c : c + 1]
            else:
                rate = edge_in[0, 6:7, :]
                base = 256 * (k - 1)
                pv = jnp.concatenate([rate[:, base : base + 128]] * (cz // 128), axis=1)
                bv = jnp.concatenate([rate[:, base + 128 : base + 256]] * (cz // 128), axis=1)
                under = (pv * own[c : c + 1] + bv * u[0:1]) * below_edge
            upper_y = jnp.where(rowz == last, own[3 + c : 4 + c], pltpu.roll(u, cy - 1, 0))
            lower_y = jnp.where(rowz == 0, under, pltpu.roll(u, 1, 0))
            slope_y = (upper_y - lower_y) * ymet[...]
            convection = -(uref[0] * slope_x + uref[1] * slope_y + uref[2] * slope_z)
            rhs = u + step * (convection + accum[c * cy : (c + 1) * cy, :])

            pa, pb, pc = thirds(rhs)
            for n, x in enumerate((pa, pb, pc, pa, pb, pa)):
                stacked[c, n * cy : (n + 1) * cy, :] = x
            solved = jnp.dot(solve_mat[k], stacked[c], preferred_element_type=F32)
            part[k, c] = solved[0:cy]
            for t in range(rsize):
                at = slice(t * width, (t + 1) * width)
                msg[k, t, c : c + 1, :] = solved[cy : cy + 1, at]
                msg[k, t, 3 + c : 4 + c, :] = solved[0:1, at]

        if k == SECTIONS - 1:
            sent, pending = pending, []
        first = []
        for d in range(1, rsize):
            to = lax.rem(place + d, rsize)
            first.append(
                send(msg.at[k, to], got1.at[k, place], s1s.at[k, d - 1], s1r.at[k, d - 1], (gx, line0 + to))
            )
        pending.extend(first)
        got1[k, place] = msg[k, place]
        if k < SECTIONS - 1:
            plane_copies = send_planes(k + 1, part.at[k])
            pending.extend(plane_copies)
            gather_plane(part.at[k], 0)
        for copy in first:
            copy.wait_recv()
        tiles = [got1[k, t] for t in range(rsize)]
        coefs = [coefficients(x) for x in tiles]
        e = jnp.where(sub == 6, 1.0, 0.0)
        starts = []
        for t in range(rsize):
            starts.append(e)
            e = down(tiles[t], coefs[t][0], e)
        l = jnp.where(sub == 7, 1.0, 0.0)
        ends = [None] * rsize
        for t in reversed(range(rsize)):
            ends[t] = l
            l = up(tiles[t], coefs[t][1], coefs[t][2], starts[t], l)
        whole = jnp.where(
            (sub < 3) | (sub == 6),
            e,
            jnp.where((sub == 7) & (col < width // 2), pltpu.roll(l, 1, 0), l),
        )
        own2[k] = whole
        got2[k, line] = whole
        second = []
        for d in range(1, rows_n):
            to = lax.rem(line + d, rows_n)
            second.append(
                send(own2.at[k], got2.at[k, line], s2s.at[k, d - 1], s2r.at[k, d - 1], (gx, to * rsize + place))
            )
        pending.extend(second)
        middle = (sub >= 3) & (sub < 6)
        forms = []
        for t in range(rsize):
            base = jnp.where(sub < 3, starts[t], jnp.where(middle, ends[t], 0.0))
            of_e = jnp.where(sub < 3, starts[t][6:7], jnp.where(middle, ends[t][6:7], 0.0))
            of_l = jnp.where(middle, ends[t][7:8], 0.0)
            forms.append((base, of_e, of_l))
        if k < SECTIONS - 1:
            rates(k + 1)
            responses(k + 1)
        else:
            while sent:
                sent.pop().wait_send()
        for copy in second:
            copy.wait_recv()
        maps = [got2[k, q] for q in range(rows_n)]
        mcoefs = [coefficients(x) for x in maps]
        e = jnp.zeros((8, width), F32)
        e_row = jnp.zeros((8, width), F32)
        starts = []
        for q in range(rows_n):
            starts.append(e)
            e_row = jnp.where(line == q, e, e_row)
            e = down(maps[q], mcoefs[q][0], e)
        l = jnp.zeros((8, width), F32)
        l_row = jnp.zeros((8, width), F32)
        for q in reversed(range(rows_n)):
            l_row = jnp.where(line == q, l, l_row)
            l = up(maps[q], mcoefs[q][1], mcoefs[q][2], starts[q], l)
        e = jnp.where(sub < 3, e_row, pltpu.roll(e_row, 3, 0))
        for t in range(rsize):
            base, of_e, of_l = forms[t]
            ans[k, t] = base + of_e * e + of_l * l_row
        third = {slot: [] for slot in range(3)}
        routes = [(0, gx), (2, west), (1, east)] if k < SECTIONS - 1 else [(0, gx)]
        for slot, column in routes:
            for d in range(1 if slot == 0 else 0, rsize):
                to = lax.rem(place + d, rsize)
                third[slot].append(
                    send(ans.at[k, to], el.at[k, slot, place], s3s.at[k, slot, d], s3r.at[k, slot, d], (column, line0 + to))
                )
        pending.extend(third[0] + third[1] + third[2])
        el[k, 0, place] = ans[k, place]
        if k < SECTIONS - 1:
            plane_copies[0].wait_recv()
            gather_plane(planes.at[k + 1, 1], 1)
        else:
            for copy in trips:
                copy.wait_recv()
            part_out[:, 0:RESIDENT] = moved[0:3, 0:RESIDENT]
            part_out[:, RESIDENT : RESIDENT + CAP] = mig[0, 0:3, :]
            part_out[:, RESIDENT + CAP : RESIDENT + 2 * CAP] = mig[1, 0:3, :] * above_edge
            part_out[:, RESIDENT + 2 * CAP : RESIDENT + 3 * CAP] = mig[2, 0:3, :] * below_edge
        for copy in third[0] + third[2]:
            copy.wait_recv()
        behind = third[1]

    rows = plane_rows(SECTIONS - 1, 0)
    k = SECTIONS - 1
    for c in range(comps):
        field_out[c] = part[k, c] + alpha[k] * rows[c : c + 1] + beta[k] * rows[3 + c : 4 + c]
    for copy in pending:
        copy.wait_send()


def finish(field, moved, field_out, moved_out, sems):
    copies = [
        pltpu.make_async_copy(field, field_out, sems.at[0]),
        pltpu.make_async_copy(moved, moved_out, sems.at[1]),
    ]
    for copy in copies:
        copy.start()
    for copy in copies:
        copy.wait()


def on_device(
    velocity, y_metric, forward_rate, backward_rate, pivot_inv,
    particle_vel, particle_cell, particle_offset, inverse_tau, outgoing_count,
):
    comps, _, cy, cz = velocity.shape
    slots = particle_vel.shape[1]
    nx, lanes = lax.axis_size("gx"), lax.axis_size("gy")
    rsize = row_size(lanes)
    rows_n = lanes // rsize
    width = cz // rsize
    vmem, smem_of = pltpu.VMEM, pltpu.SMEM
    whole = pl.BlockSpec(memory_space=pltpu.VMEM)
    dma = pltpu.SemaphoreType.DMA
    far = pl.BlockSpec(memory_space=pltpu.HBM)

    def stay(x):
        return pltpu.with_memory_space_constraint(x, pltpu.HBM)

    scratch = [
        vmem((comps, cy, cz), F32), vmem((comps, slots), F32), vmem((slots,), jnp.int32),
        vmem((3, slots), F32), vmem((slots,), F32), dma((10,)),
        smem_of((cy,), F32), smem_of((SECTIONS, cy), F32), smem_of((SECTIONS, cy), F32),
        smem_of((SECTIONS, cy), F32), smem_of((3,), jnp.int32),
        vmem((cz, slots), BF16),
        vmem((slots, cz), BF16),
        vmem((4 * comps * cy + 64, cz), BF16),
        vmem((2 * comps * cy, slots), BF16),
        vmem((comps * cy, cz), F32),
        vmem((8, slots), F32),
        vmem((cy, slots), F32),
        vmem((cy, slots), F32),
        vmem((8, slots), F32),
        vmem((8, slots), F32),
        vmem((8, slots), F32),
        vmem((1, slots), F32),
        vmem((8, slots), F32),
        vmem((SECTIONS, 2 * cy, 128), BF16),
        vmem((comps, 128, cz), BF16),
        vmem((SECTIONS, cy, cz), F32),
        vmem((SECTIONS, cy, cz), F32),
        vmem((cy, cz), F32),
        vmem((cy, 128), F32),
        vmem((SECTIONS, comps, cy, cz), F32),
        vmem((SECTIONS, 2, comps, cy, cz), F32),
        vmem((comps, cy, cz), F32),
        vmem((8, cz), F32),
        vmem((3, 8, cz), F32),
        vmem((SECTIONS, rsize, 8, width), F32),
        vmem((SECTIONS, rsize, 8, width), F32),
        vmem((SECTIONS, rows_n, 8, width), F32),
        vmem((SECTIONS, 8, width), F32),
        vmem((SECTIONS, rsize, 8, width), F32),
        vmem((SECTIONS, 3, rsize, 8, width), F32),
        vmem((3, 8, CAP), F32),
        dma((SECTIONS, rsize - 1)), dma((SECTIONS, rsize - 1)),
        dma((SECTIONS, rows_n - 1)), dma((SECTIONS, rows_n - 1)),
        dma((SECTIONS, 3, rsize)), dma((SECTIONS, 3, rsize)),
        dma((SECTIONS, 2)), dma((SECTIONS, 2)),
        dma((3,)), dma((3,)), dma((3,)), dma((3,)),
    ]
    field, moved = pl.pallas_call(
        functools.partial(kernel, (nx, lanes, rsize)),
        out_shape=(
            jax.ShapeDtypeStruct((comps, cy, cz), F32),
            jax.ShapeDtypeStruct((comps, slots), F32),
        ),
        in_specs=[far] * 10,
        out_specs=(whole, whole),
        scratch_shapes=scratch,
        compiler_params=pltpu.CompilerParams(
            collective_id=0, has_side_effects=True, vmem_limit_bytes=48 * 1024 * 1024
        ),
        name="channel_sections",
    )(
        stay(velocity.reshape(comps, cy, cz)),
        stay(y_metric),
        stay(forward_rate),
        stay(backward_rate),
        stay(pivot_inv),
        stay(particle_vel),
        stay(particle_cell),
        stay(particle_offset),
        stay(inverse_tau),
        stay(outgoing_count.reshape(3)),
    )
    field, moved = pl.pallas_call(
        finish,
        out_shape=(
            jax.ShapeDtypeStruct((comps, cy, cz), F32),
            jax.ShapeDtypeStruct((comps, slots), F32),
        ),
        in_specs=[whole, whole],
        out_specs=(far, far),
        scratch_shapes=[dma((2,))],
        compiler_params=pltpu.CompilerParams(vmem_limit_bytes=4 * 1024 * 1024),
        name="write_out",
    )(field, moved)
    return field.reshape(velocity.shape), moved


def solution(mesh):
    return jax.shard_map(
        on_device,
        mesh=mesh,
        in_specs=(
            P(None, "gx", "gy", None),
            P("gy"),
            P(None, "gy"),
            P(None, "gy"),
            P(None, "gy"),
            P(None, ("gx", "gy")),
            P(("gx", "gy")),
            P(None, ("gx", "gy")),
            P(("gx", "gy")),
            P("gx", "gy", None),
        ),
        out_specs=(P(None, "gx", "gy", None), P(None, ("gx", "gy"))),
        check_vma=False,
    )
```
